128 devices in a mesh: grp: 2 (over core), pts: 64 (over x, z, y).
Axes of the slice: x: 4, y: 4, z: 4, core: 2. Of those that a mesh axis runs over, the one named last changes fastest.
Arguments:
- points_z: bfloat16 [131072, 256], P(('grp', 'pts')), may hold values from -40 to 40
- patch_len: int32 [128], P(('grp', 'pts')), may hold values from 961 to 1024
- z_dest: int32 [1024], P(('grp', 'pts')), may hold values from 0 to 1023, as said below
- cell_of: int32 [131072], P(('grp', 'pts')), may hold values from 0 to 32767, as said below
- norm_gain: float32 [2, 2, 256], replicated, may hold values from 0.25 to 1.75
- qkv_weight: bfloat16 [2, 256, 768], replicated, may hold values from -8 to 8
- out_weight: bfloat16 [2, 256, 256], replicated, may hold values from -0.375 to 0.375
- up_weight: bfloat16 [2, 256, 1024], replicated, may hold values from -0.375 to 0.375
- down_weight: bfloat16 [2, 1024, 256], replicated, may hold values from -0.1875 to 0.1875
- pool_weight: bfloat16 [256, 512], replicated, may hold values from -0.375 to 0.375
Outputs:
- pooled: bfloat16 [32768, 512], P(('grp', 'pts'))
The draws below stay inside these ranges and needn't reach their ends.
Inputs may be any that keep to these rules, and one draw needn't show every extreme that they name: z_dest is a permutation of the block numbers. With devices taken in the order grp then pts, cyclically, and D their number, a block of the device of index i goes to the device of index i + delta, where the set of deltas is the same on every device: every value from -4 + 1 to 3, and D / 2; each delta is taken by exactly 1 block of a device. cell_of never falls along the points in the order grp then pts. Each device starts exactly 256 cells, numbered from its index times 256; its points before its first start belong to the last cell of the previous device; the first point of all starts cell 0.
All inputs are finite; a program needn't handle non-finite values.
Results may differ from the reference program's by a relative error of at most 0.012.
Values may be sent and summed in bfloat16 or wider, within the bound.
A program may use at most 64 MiB of HBM per device.

```python
import jax
import jax.numpy as jnp
from jax import lax

C = 256
HEADS = 16
FF = 1024
CP = 512
PATCH = 1024
BLK = 128
REACH = 4
P_DEV = 1024
BLK_DEV = 8
CELL_DEV = 256
POINTS = 131072
PATCHES = 128
NBLK = 1024
CELLS = 32768
N_GRP = 2
N_PTS = 64


def draw_z_dest(key, part):
    devices = N_GRP * N_PTS
    per_pair = BLK_DEV // (2 * REACH)
    key_send = jax.random.fold_in(key, 1)
    key_take = jax.random.fold_in(key, 2)

    def shuffled(subkey):
        return jax.random.permutation(subkey, BLK_DEV)
    far_step = jnp.full((1,), devices // 2, jnp.int32)
    inner_steps = (jnp.arange(2 * REACH - 1) - (REACH - 1)).astype(jnp.int32)
    offsets = jnp.concatenate([inner_steps, far_step]).astype(jnp.int32)
    sender_order = jax.vmap(shuffled)(jax.random.split(key_send, devices))
    taker_order = jax.vmap(shuffled)(jax.random.split(key_take, devices))
    source = jnp.arange(devices)[:, None]
    target = (source + offsets[sender_order // per_pair]) % devices
    slot_index = taker_order[target, sender_order]
    return (target * BLK_DEV + slot_index).reshape(devices * BLK_DEV).astype(jnp.int32)


def draw_cell_of(key, part):
    devices = N_GRP * N_PTS

    def shuffled(subkey):
        return jax.random.permutation(subkey, P_DEV)
    shuffled_ranks = jax.vmap(shuffled)(jax.random.split(key, devices))
    first_row = shuffled_ranks[0]
    zero_at = jnp.argmax(first_row == 0)
    first_row = first_row.at[zero_at].set(first_row[0]).at[0].set(0)
    shuffled_ranks = shuffled_ranks.at[0].set(first_row)
    starts = (shuffled_ranks < CELL_DEV).astype(jnp.int32)
    cell_ids = jnp.cumsum(starts, axis=1) - 1 + jnp.arange(devices)[:, None] * CELL_DEV
    return cell_ids.reshape(devices * P_DEV).astype(jnp.int32)


def draw_points_z(key, part):
    key_base = jax.random.fold_in(key, 0)
    return jnp.clip(jax.random.normal(key_base, (POINTS, C), jnp.float32), -6.0, 6.0).astype(jnp.bfloat16)


def draw_qkv_weight(key, part):
    key_query, key_keys, key_value = jax.random.split(key, 3)
    deviation = C ** (-0.5)
    query_part = jax.random.normal(key_query, (2, C, C), jnp.float32) * deviation
    key_part = jax.random.normal(key_keys, (2, C, C), jnp.float32) * deviation
    value_part = jax.random.normal(key_value, (2, C, C), jnp.float32) * deviation
    return jnp.concatenate([query_part, key_part, value_part], axis=2).astype(jnp.bfloat16)


def touch_ends(values, key, least, largest):
    place = [jax.random.randint(jax.random.fold_in(key, axis), (), 0, length) for axis, length in enumerate(values.shape)]
    longest = values.shape.index(max(values.shape))
    neighbour = place[:longest] + [(place[longest] + 1) % values.shape[longest]] + place[longest + 1:]
    return values.at[tuple(place)].set(least).at[tuple(neighbour)].set(largest)


def noise(stream_key, dims, scale, limit, dtype=jnp.bfloat16):
    values = scale * jax.random.normal(stream_key, dims, jnp.float32)
    return jnp.clip(values, min=-limit, max=limit).astype(dtype)


def setup_inputs(seed: int = 0) -> dict:
    splits = jax.random.split(jax.random.key(seed), 11)
    points_z = draw_points_z(jax.random.fold_in(splits[10], 71), 0)
    patch_len = touch_ends(jax.random.randint(splits[1], (PATCHES,), PATCH - BLK // 2 + 1, PATCH + 1), jax.random.fold_in(splits[1], 1), PATCH - BLK // 2 + 1, PATCH).astype(jnp.int32)
    z_dest = draw_z_dest(jax.random.fold_in(splits[10], 71), 0)
    cell_of = draw_cell_of(jax.random.fold_in(splits[10], 71), 0)
    norm_gain = jnp.clip(1.0 + 0.15 * jax.random.normal(splits[4], (2, 2, C), jnp.float32), 0.25, 1.75)
    qkv_weight = draw_qkv_weight(jax.random.fold_in(splits[10], 71), 0)
    out_weight = noise(splits[6], (2, C, C), C ** -0.5, 0.375)
    up_weight = noise(splits[7], (2, C, FF), C ** -0.5, 0.375)
    down_weight = noise(splits[8], (2, FF, C), FF ** -0.5, 0.1875)
    pool_weight = noise(splits[9], (C, CP), C ** -0.5, 0.375)
    return dict(points_z=points_z, patch_len=patch_len, z_dest=z_dest, cell_of=cell_of, norm_gain=norm_gain, qkv_weight=qkv_weight, out_weight=out_weight, up_weight=up_weight, down_weight=down_weight, pool_weight=pool_weight)


NORM_EPS = 1e-05

def stored(values):
    return lax.optimization_barrier(values.astype(jnp.bfloat16))

def normalize(features, gain_row):
    widened = features.astype(jnp.float32)
    centered = widened - lax.optimization_barrier(jnp.mean(widened, axis=-1, keepdims=True))
    variance = lax.optimization_barrier(jnp.mean(centered * centered, axis=-1, keepdims=True))
    return (centered * lax.rsqrt(variance + NORM_EPS) * gain_row).astype(jnp.bfloat16)

def patch_attention(projected, key_live):
    head_size = C // HEADS
    queries = projected[:, :C].reshape(PATCH, HEADS, head_size).astype(jnp.float32)
    keys_all = projected[:, C:2 * C].reshape(PATCH, HEADS, head_size).astype(jnp.float32)
    values = projected[:, 2 * C:].reshape(PATCH, HEADS, head_size).astype(jnp.float32)
    scores = jnp.einsum('qhd,khd->hqk', queries, keys_all) * head_size ** (-0.5)
    scores = jnp.where(key_live[None, None, :] > 0, scores, -jnp.inf)
    row_max = lax.optimization_barrier(jnp.max(scores, axis=-1, keepdims=True))
    weights = jnp.exp(scores - row_max)
    denominator = lax.optimization_barrier(jnp.sum(weights, axis=-1))
    rounded = stored(weights).astype(jnp.float32)
    attended = jnp.einsum('hqk,khd->qhd', rounded, values) / denominator.T[:, :, None]
    return stored(attended).reshape(PATCH, C)

def transformer_block(points, key_live, gain_pair, qkv_weights, out_weights, up_weights, down_weights):
    normed = normalize(points, gain_pair[0])
    projected = stored(jnp.dot(normed, qkv_weights, preferred_element_type=jnp.float32))
    attended = patch_attention(projected, key_live)
    residual = stored(points.astype(jnp.float32) + jnp.dot(attended, out_weights, preferred_element_type=jnp.float32))
    hidden = stored(jax.nn.gelu(jnp.dot(normalize(residual, gain_pair[1]), up_weights, preferred_element_type=jnp.float32), approximate=False))
    return stored(residual.astype(jnp.float32) + jnp.dot(hidden, down_weights, preferred_element_type=jnp.float32))

def run_block(points, key_live, gain_pair, qkv_weights, out_weights, up_weights, down_weights):
    shaped = points.reshape(-1, PATCH, C)
    live_rows = key_live.reshape(-1, PATCH)

    def one_patch(entries):
        return transformer_block(entries[0], entries[1], gain_pair, qkv_weights, out_weights, up_weights, down_weights)
    return lax.map(one_patch, (shaped, live_rows)).reshape(-1, C)

def reference(points_z, patch_len, z_dest, cell_of, norm_gain, qkv_weight, out_weight, up_weight, down_weight, pool_weight):
    position = jnp.arange(POINTS) % PATCH
    keep_z = (position < jnp.repeat(patch_len, PATCH)).astype(jnp.int32)
    first = run_block(points_z, keep_z, norm_gain[0], qkv_weight[0], out_weight[0], up_weight[0], down_weight[0])
    moved = jnp.zeros((NBLK, BLK, C), jnp.bfloat16).at[z_dest].set(first.reshape(NBLK, BLK, C))
    regrouped = moved.reshape(POINTS, C)
    keep_h = jnp.zeros((NBLK, BLK), jnp.int32).at[z_dest].set(keep_z.reshape(NBLK, BLK)).reshape(POINTS)
    second = run_block(regrouped, keep_h, norm_gain[1], qkv_weight[1], out_weight[1], up_weight[1], down_weight[1])
    live_rows = keep_h.astype(jnp.float32)
    cell_sums = jax.ops.segment_sum(second.astype(jnp.float32) * live_rows[:, None], cell_of, num_segments=CELLS)
    counts = jax.ops.segment_sum(live_rows, cell_of, num_segments=CELLS)
    mean_rows = stored(cell_sums / jnp.maximum(counts, 1.0)[:, None])
    return stored(jax.nn.gelu(jnp.dot(mean_rows, pool_weight, preferred_element_type=jnp.float32), approximate=False))
```

```python
import functools

import jax
import jax.numpy as jnp
from jax import lax
from jax.experimental import pallas as pl
from jax.experimental.pallas import tpu as pltpu
from jax.sharding import PartitionSpec as P

C = 256
HEADS = 16
HD = 16
PATCH = 1024
BLK = 128
NB = 8
CELL_DEV = 256
CP = 512
FF = 1024
NORM_EPS = 1e-05
QW = 512
ROWS = 256
LOG2E = 1.4426950408889634
POOL_ROWS = 272
ERF = (
    0.7978722361090334,
    0.03636660609986694,
    -5.8514434084682766e-05,
    -4.7090980998381986e-05,
    2.779316469575001e-06,
    -5.589976858483281e-08,
)
ERF_END = 5.6 * 5.6
bf16 = jnp.bfloat16
f32 = jnp.float32
MESH = pl.DeviceIdType.MESH


def gelu(x):
    u = jnp.minimum(x * x, ERF_END)
    r = ERF[5]
    for coefficient in ERF[4::-1]:
        r = r * u + coefficient
    half = 0.5 * x
    return half + half * jnp.tanh(x * r)


def norm(x, gain):
    centered = x - jnp.mean(x, axis=-1, keepdims=True)
    variance = jnp.mean(centered * centered, axis=-1, keepdims=True)
    return (centered * lax.rsqrt(variance + NORM_EPS) * gain).astype(bf16)


def dot(a, b):
    return jnp.dot(a, b, preferred_element_type=f32)


def dot_nt(a, b):
    return lax.dot_general(a, b, (((1,), (1,)), ((), ())), preferred_element_type=f32)


def dot_tn(a, b):
    return lax.dot_general(a, b, (((0,), (0,)), ((), ())), preferred_element_type=f32)


def project(b, chunk, xs, meta, gain, wqkv, wqv_t, kk, qt, vt):
    rows = pl.ds(chunk * ROWS, ROWS)
    xn = norm(xs[rows, :].astype(f32), gain[b, 0:1, :])
    k = dot(xn, wqkv[b, :, C : 2 * C])
    for part in range(2):
        slot = chunk * 2 + part
        limit = meta[slot, 1:2, :]
        live = lax.broadcasted_iota(jnp.int32, (BLK, C), 0) < limit
        piece = k[part * BLK : (part + 1) * BLK, :]
        piece = jnp.where(live, piece, piece[0:1, :]).astype(bf16)
        at = pl.ds(slot * BLK, BLK)
        for g in range(2):
            lanes = piece[:, g * 128 : (g + 1) * 128]
            kk[g, at, 0:128] = lanes
            kk[g, at, 128:256] = lanes
    qv = dot_nt(wqv_t[...], xn)
    q = qv[:C, :].astype(bf16).astype(f32) * (HD**-0.5 * LOG2E)
    hi = q.astype(bf16)
    lo = (q - hi.astype(f32)).astype(bf16)
    for h in range(HEADS):
        r = (h % 8) * HD
        qt[h, r : r + HD, rows] = hi[h * HD : (h + 1) * HD, :]
        qt[h, 128 + r : 128 + r + HD, rows] = lo[h * HD : (h + 1) * HD, :]
    limits = jnp.concatenate(
        [meta[chunk * 2, 1:2, 0:BLK], meta[chunk * 2 + 1, 1:2, 0:BLK]], axis=1
    )
    lane = lax.broadcasted_iota(jnp.int32, (1, ROWS), 1) % BLK
    live_row = (lane < limits).astype(f32)
    v = (qv[C:, :] * live_row).astype(bf16)
    first = lax.broadcasted_iota(jnp.int32, (HD, ROWS), 0) == 0
    ones = jnp.where(first, live_row, 0.0).astype(bf16)
    for h in range(HEADS):
        vt[h, 0:HD, rows] = v[h * HD : (h + 1) * HD, :]
        vt[h, HD : 2 * HD, rows] = ones


def attention(kk, qt, vt, ot, s_a, s_b, m_a, m_b):
    tiles = PATCH // QW

    def scores(h, t, s, m):
        raw = dot(kk[h // 8], qt[h, :, pl.ds(t * QW, QW)])
        s[...] = raw
        m[...] = jnp.max(raw.reshape(PATCH // 8, 8, QW), axis=0)

    def values(h, t, s, m):
        top = jnp.max(m[...], axis=0, keepdims=True)
        total = None
        for c in range(PATCH // 256):
            keys = pl.ds(c * 256, 256)
            e = jnp.exp2(s[keys, :] - top).astype(bf16)
            part = dot(vt[h, :, keys], e)
            total = part if total is None else total + part
        ot[pl.ds(pl.multiple_of(h * HD, HD), HD), pl.ds(t * QW, QW)] = (
            total[0:HD, :] / total[HD : HD + 1, :]
        ).astype(bf16)

    scores(0, 0, s_a, m_a)

    def head(h, carry):
        for t in range(tiles):
            now = (s_a, m_a) if t % 2 == 0 else (s_b, m_b)
            later = (s_b, m_b) if t % 2 == 0 else (s_a, m_a)
            next_h = h if t < tiles - 1 else jnp.minimum(h + 1, HEADS - 1)
            scores(next_h, (t + 1) % tiles, *later)
            values(h, t, *now)
        return carry

    lax.fori_loop(0, HEADS, head, 0)


def finish(b, chunk, xs, gain, ot, wo, wup, wdown):
    rows = pl.ds(chunk * ROWS, ROWS)
    h = xs[rows, :].astype(f32) + dot_tn(ot[:, rows], wo[b])
    h = h.astype(bf16).astype(f32)
    hn = norm(h, gain[b, 1:2, :])
    u = gelu(dot(hn, wup[b])).astype(bf16)
    return (h + dot(u, wdown[b])).astype(bf16)


def transpose_weights(b, wqkv, wqv_t):
    for part, first in enumerate((0, 2 * C)):
        w = wqkv[b, :, first : first + C].astype(f32)
        wqv_t[part * C : (part + 1) * C, :] = w.T.astype(bf16)


def body(
    deltas,
    devices,
    n_pts,
    patch_len,
    z_dest,
    x_ref,
    cells,
    gain,
    wqkv,
    wo,
    wup,
    wdown,
    wpool,
    out,
    x_first,
    x_second,
    y_send,
    wqv_t,
    kk,
    qt,
    vt,
    ot,
    s_a,
    s_b,
    m_a,
    m_b,
    meta_send,
    meta_recv,
    rim_send,
    rim_recv,
    send_sem,
    recv_sem,
    meta_send_sem,
    meta_recv_sem,
    rim_send_sem,
    rim_recv_sem,
):
    me = lax.axis_index("grp") * n_pts + lax.axis_index("pts")

    def device(delta):
        flat = (me + delta + devices) % devices
        return (flat // n_pts, flat % n_pts)

    barrier = pltpu.get_barrier_semaphore()
    for delta in deltas:
        if delta:
            pl.semaphore_signal(barrier, inc=1, device_id=device(delta), device_id_type=MESH)
    pl.semaphore_wait(barrier, NB - 1)

    def remote(src, dst, ssem, rsem, delta):
        return pltpu.make_async_remote_copy(
            src_ref=src, dst_ref=dst, send_sem=ssem, recv_sem=rsem,
            device_id=device(delta), device_id_type=MESH,
        )

    def block_copy(slot):
        rows = pl.ds(slot * BLK, BLK)
        return remote(
            y_send.at[rows], x_second.at[rows], send_sem.at[slot], recv_sem.at[slot], deltas[slot]
        )

    def meta_copy(slot):
        return remote(
            meta_send.at[slot], meta_recv.at[slot], meta_send_sem.at[slot],
            meta_recv_sem.at[slot], deltas[slot],
        )

    row = lax.broadcasted_iota(jnp.int32, (8, C), 0)
    for slot, delta in enumerate(deltas):
        base = ((me + delta + devices) % devices) * NB
        block = jnp.int32(0)
        place = jnp.int32(0)
        for n in range(NB):
            offset = z_dest[n] - base
            hit = jnp.logical_and(offset >= 0, offset < NB)
            block = block + jnp.where(hit, n, 0)
            place = place + jnp.where(hit, offset, 0)
        block = jnp.minimum(block, NB - 1)
        x_first[pl.ds(slot * BLK, BLK), :] = x_ref[block]
        limit = patch_len[0] - block * BLK
        meta = jnp.where(row == 1, limit, place)
        meta_send[slot] = meta
        if delta == 0:
            meta_recv[slot] = meta
    qt[...] = jnp.zeros_like(qt)
    for slot, delta in enumerate(deltas):
        if delta:
            meta_copy(slot).start()

    chunks = PATCH // ROWS
    transpose_weights(0, wqkv, wqv_t)
    for chunk in range(chunks):
        project(0, chunk, x_first, meta_send, gain, wqkv, wqv_t, kk, qt, vt)
    attention(kk, qt, vt, ot, s_a, s_b, m_a, m_b)
    for chunk in range(chunks):
        y = finish(0, chunk, x_first, gain, ot, wo, wup, wdown)
        for part in range(2):
            slot = chunk * 2 + part
            rows = pl.ds(slot * BLK, BLK)
            piece = y[part * BLK : (part + 1) * BLK, :]
            if deltas[slot]:
                y_send[rows, :] = piece
                block_copy(slot).start()
            else:
                x_second[rows, :] = piece

    transpose_weights(1, wqkv, wqv_t)
    for slot, delta in enumerate(deltas):
        if delta:
            meta_copy(slot).wait()
    for chunk in range(chunks):
        for slot in (chunk * 2, chunk * 2 + 1):
            if deltas[slot]:
                block_copy(slot).wait()
        project(1, chunk, x_second, meta_recv, gain, wqkv, wqv_t, kk, qt, vt)
    attention(kk, qt, vt, ot, s_a, s_b, m_a, m_b)

    number = lax.broadcasted_iota(jnp.int32, (POOL_ROWS, BLK), 0)
    wanted = jnp.where(number == CELL_DEV, -1, jnp.where(number > CELL_DEV, -5, number))
    lane = lax.broadcasted_iota(jnp.int32, (1, BLK), 1)
    ones = jnp.ones((ROWS, 128), bf16)
    sums = jnp.zeros((POOL_ROWS, C), f32)
    counts = jnp.zeros((POOL_ROWS, 128), f32)
    for chunk in range(chunks):
        y = finish(1, chunk, x_second, gain, ot, wo, wup, wdown)
        members = []
        for slot in (chunk * 2, chunk * 2 + 1):
            place = meta_recv[slot, 0:1, 0:BLK]
            cell = jnp.zeros((1, BLK), jnp.int32)
            for n in range(NB):
                cell = cell + jnp.where(place == n, cells[n : n + 1, :], 0)
            cell = jnp.where(lane < meta_recv[slot, 1:2, 0:BLK], cell - me * CELL_DEV, -9)
            members.append((cell == wanted).astype(f32).astype(bf16))
        member = jnp.concatenate(members, axis=1)
        sums = sums + dot(member, y)
        counts = counts + dot(member, ones)

    rim_send[:, 0:C] = sums[CELL_DEV : CELL_DEV + 8, :]
    rim_send[:, C : C + 128] = counts[CELL_DEV : CELL_DEV + 8, :]
    rim = remote(rim_send, rim_recv, rim_send_sem, rim_recv_sem, -1)
    rim.start()

    def pooled(total, count):
        count = jnp.maximum(count, 1.0)
        mean = total / jnp.concatenate([count, count], axis=1)
        return gelu(dot(mean.astype(bf16), wpool[...])).astype(bf16)

    out[...] = pooled(sums[:CELL_DEV, :], counts[:CELL_DEV, :])
    rim.wait()
    tail = CELL_DEV - 16
    last = lax.broadcasted_iota(jnp.int32, (16, 1), 0) == 15
    extra = jnp.where(last, rim_recv[0:1, 0:C], 0.0)
    extra_count = jnp.where(last, rim_recv[0:1, C : C + 128], 0.0)
    out[tail:, :] = pooled(
        sums[tail:CELL_DEV, :] + extra, counts[tail:CELL_DEV, :] + extra_count
    )


def on_device(
    points_z,
    patch_len,
    z_dest,
    cell_of,
    norm_gain,
    qkv_weight,
    out_weight,
    up_weight,
    down_weight,
    pool_weight,
):
    n_pts = lax.axis_size("pts")
    devices = lax.axis_size(("grp", "pts"))
    deltas = (3, -3, 2, -2, 1, -1, devices // 2, 0)
    vmem = pl.BlockSpec(memory_space=pltpu.VMEM)
    smem = pl.BlockSpec(memory_space=pltpu.SMEM)
    return pl.pallas_call(
        functools.partial(body, deltas, devices, n_pts),
        out_shape=jax.ShapeDtypeStruct((CELL_DEV, CP), bf16),
        in_specs=[smem, smem] + [vmem] * 8,
        out_specs=vmem,
        scratch_shapes=[
            pltpu.VMEM((PATCH, C), bf16),
            pltpu.VMEM((PATCH, C), bf16),
            pltpu.VMEM((PATCH, C), bf16),
            pltpu.VMEM((2 * C, C), bf16),
            pltpu.VMEM((2, PATCH, C), bf16),
            pltpu.VMEM((HEADS, C, PATCH), bf16),
            pltpu.VMEM((HEADS, 2 * HD, PATCH), bf16),
            pltpu.VMEM((C, PATCH), bf16),
            pltpu.VMEM((PATCH, QW), f32),
            pltpu.VMEM((PATCH, QW), f32),
            pltpu.VMEM((8, QW), f32),
            pltpu.VMEM((8, QW), f32),
            pltpu.VMEM((NB, 8, C), jnp.int32),
            pltpu.VMEM((NB, 8, C), jnp.int32),
            pltpu.VMEM((8, C + 128), f32),
            pltpu.VMEM((8, C + 128), f32),
            pltpu.SemaphoreType.DMA((NB,)),
            pltpu.SemaphoreType.DMA((NB,)),
            pltpu.SemaphoreType.DMA((NB,)),
            pltpu.SemaphoreType.DMA((NB,)),
            pltpu.SemaphoreType.DMA,
            pltpu.SemaphoreType.DMA,
        ],
        compiler_params=pltpu.CompilerParams(
            collective_id=0, has_side_effects=True, vmem_limit_bytes=48 * 2**20
        ),
        name="encoder",
    )(
        patch_len,
        z_dest,
        points_z.reshape(NB, BLK, C),
        cell_of.reshape(NB, BLK),
        norm_gain,
        qkv_weight,
        out_weight,
        up_weight,
        down_weight,
        pool_weight,
    )


def solution(mesh):
    placed = (
        P(("grp", "pts"), None),
        P(("grp", "pts")),
        P(("grp", "pts")),
        P(("grp", "pts")),
        P(),
        P(),
        P(),
        P(),
        P(),
        P(),
    )
    return jax.shard_map(
        on_device, mesh=mesh, in_specs=placed, out_specs=P(("grp", "pts"), None), check_vma=False
    )
```

```python
import functools

import jax
import jax.numpy as jnp
from jax import lax
from jax.experimental import pallas as pl
from jax.experimental.pallas import tpu as pltpu
from jax.sharding import PartitionSpec as P

C = 256
HEADS = 16
HD = 16
PATCH = 1024
BLK = 128
NB = 8
CELL_DEV = 256
CP = 512
FF = 1024
NORM_EPS = 1e-05
QW = 512
ROWS = 256
LOG2E = 1.4426950408889634
POOL_ROWS = 272
ERF = (
    0.7978281360364785,
    0.03646879080750627,
    -0.00012486153426078468,
    -3.0581026877848916e-05,
    1.1190833948473977e-06,
)
F8_TOP = 400.0
bf16 = jnp.bfloat16
f8 = jnp.float8_e4m3fn
f32 = jnp.float32
MESH = pl.DeviceIdType.MESH


def gelu(x):
    u = x * x
    r = ERF[4]
    for coefficient in ERF[3::-1]:
        r = r * u + coefficient
    half = 0.5 * x
    return half + half * jnp.tanh(x * r)


def norm(x, gain):
    centered = x - jnp.mean(x, axis=-1, keepdims=True)
    variance = jnp.mean(centered * centered, axis=-1, keepdims=True)
    return (centered * lax.rsqrt(variance + NORM_EPS) * gain).astype(bf16)


def dot(a, b):
    return jnp.dot(a, b, preferred_element_type=f32)


def dot_nt(a, b):
    return lax.dot_general(a, b, (((1,), (1,)), ((), ())), preferred_element_type=f32)


def dot_tn(a, b):
    return lax.dot_general(a, b, (((0,), (0,)), ((), ())), preferred_element_type=f32)


def prepare(b, gain, wqkv, wq_t, wk2, sigma):
    reach = 16.1 * jnp.max(jnp.abs(gain[b, 0:1, :]))
    column = lax.broadcasted_iota(jnp.int32, (C, C), 0) // HD
    same_head = (column == lax.broadcasted_iota(jnp.int32, (C, C), 1) // HD).astype(f32).astype(bf16)

    def power(exponent):
        return jnp.exp2(exponent).astype(bf16).astype(f32)

    def exponents(w):
        squares = jnp.sum(w * w, axis=0, keepdims=True)
        squares = jnp.broadcast_to(squares, (16, C)).astype(bf16)
        total = jnp.maximum(dot(squares, same_head)[0:1, :], 1e-30)
        bound = reach * jnp.sqrt(total)
        return jnp.floor(jnp.log(F8_TOP / bound) * LOG2E)

    wq = wqkv[b, :, 0:C].astype(f32)
    wk = wqkv[b, :, C : 2 * C].astype(f32)
    wv = wqkv[b, :, 2 * C : 3 * C].astype(f32)
    q_up, k_up = exponents(wq), exponents(wk)
    wq_t[0:C, :] = (wq * power(q_up)).T.astype(bf16)
    wq_t[C : 2 * C, :] = wv.T.astype(bf16)
    column = lax.broadcasted_iota(jnp.int32, (C, 2 * C), 0)
    wide = lax.broadcasted_iota(jnp.int32, (C, 2 * C), 1)
    twice = (column == (wide // (2 * HD)) * HD + wide % HD).astype(f32).astype(bf16)
    wk2[...] = dot((wk * power(k_up)).astype(bf16), twice).astype(bf16)
    back = power(-q_up - k_up) * (HD**-0.5 * LOG2E)
    for h in range(HEADS):
        sigma[h] = jnp.broadcast_to(back[:, h * HD : h * HD + 1], (8, QW))


def project(b, chunk, xs, meta, gain, wq_t, wk2, kk, qt, vt, spare):
    rows = pl.ds(chunk * ROWS, ROWS)
    xn = norm(xs[rows, :].astype(f32), gain[b, 0:1, :])
    k = dot(xn, wk2[...]).astype(bf16).astype(f32)
    is_high = lax.broadcasted_iota(jnp.int32, (BLK, 2 * C), 1) % (2 * HD) < HD
    for part in range(2):
        slot = chunk * 2 + part
        limit = meta[slot, 1:2, :]
        limit = jnp.concatenate([limit, limit], axis=1)
        spare[slot : slot + 1, :] = (BLK - jnp.minimum(limit, BLK)).astype(f32)
        live = lax.broadcasted_iota(jnp.int32, (BLK, 2 * C), 0) < limit
        piece = k[part * BLK : (part + 1) * BLK, :]
        piece = jnp.where(live, piece, piece[0:1, :])
        high = piece.astype(f8).astype(f32)
        piece = jnp.where(is_high, high, piece - high).astype(f8)
        for g in range(4):
            kk[g, pl.ds(slot * BLK, BLK), :] = piece[:, g * 128 : (g + 1) * 128]
    qv = dot_nt(wq_t[...], xn)
    q = qv[:C, :].astype(bf16).astype(f32)
    high = q.astype(f8).astype(f32)
    low = q - high
    for h in range(HEADS):
        r = (h % 4) * 2 * HD
        at = slice(h * HD, (h + 1) * HD)
        qt[h, r : r + 2 * HD, rows] = jnp.concatenate([high[at], high[at]], axis=0).astype(f8)
        qt[h, 128 + r : 128 + r + 2 * HD, rows] = jnp.concatenate(
            [low[at], low[at]], axis=0
        ).astype(f8)
    limits = jnp.concatenate(
        [meta[chunk * 2, 1:2, 0:BLK], meta[chunk * 2 + 1, 1:2, 0:BLK]], axis=1
    )
    lane = lax.broadcasted_iota(jnp.int32, (1, ROWS), 1) % BLK
    v = (qv[C:, :] * (lane < limits).astype(f32)).astype(bf16)
    for h in range(HEADS):
        vt[h, :, rows] = v[h * HD : (h + 1) * HD, :]


def attention(kk, qt, vt, ot, sigma, spare, s_a, s_b, m_a, m_b):
    tiles = PATCH // QW

    def scores(h, t, s, m):
        keys = kk[h // 4]
        raw = dot(jnp.concatenate([keys, keys], axis=1), qt[h, :, pl.ds(t * QW, QW)])
        s[...] = raw
        m[...] = jnp.max(raw.reshape(PATCH // 8, 8, QW), axis=0)

    def values(h, t, s, m):
        scale = sigma[h][0:1, :]
        top = jnp.max(m[...], axis=0, keepdims=True) * scale
        total = None
        for c in range(PATCH // 256):
            keys = pl.ds(c * 256, 256)
            e = jnp.exp2(s[keys, :] * scale - top)
            part = dot(vt[h, :, keys], e.astype(bf16))
            count = jnp.sum(e.reshape(32, 8, QW), axis=0)
            over = spare[2 * c : 2 * c + 1, :] * e[0:1] + spare[2 * c + 1 : 2 * c + 2, :] * e[BLK : BLK + 1]
            if total is None:
                total, counted, left_out = part, count, over
            else:
                total, counted, left_out = total + part, counted + count, left_out + over
        den = jnp.sum(counted, axis=0, keepdims=True) - left_out
        ot[pl.ds(pl.multiple_of(h * HD, HD), HD), pl.ds(t * QW, QW)] = (total / den).astype(bf16)

    scores(0, 0, s_a, m_a)

    def head(h, carry):
        for t in range(tiles):
            now = (s_a, m_a) if t % 2 == 0 else (s_b, m_b)
            later = (s_b, m_b) if t % 2 == 0 else (s_a, m_a)
            next_h = h if t < tiles - 1 else jnp.minimum(h + 1, HEADS - 1)
            scores(next_h, (t + 1) % tiles, *later)
            values(h, t, *now)
        return carry

    lax.fori_loop(0, HEADS, head, 0)


def residual(b, chunk, xs, gain, ot, wo, hs, hns):
    rows = pl.ds(chunk * ROWS, ROWS)
    h = (xs[rows, :].astype(f32) + dot_tn(ot[:, rows], wo[b])).astype(bf16)
    hs[rows, :] = h
    hns[rows, :] = norm(h.astype(f32), gain[b, 1:2, :])


def feed_forward(b, chunk, hs, hns, wup, wdown):
    rows = pl.ds(chunk * ROWS, ROWS)
    u = gelu(dot(hns[rows, :], wup[b])).astype(bf16)
    return (hs[rows, :].astype(f32) + dot(u, wdown[b])).astype(bf16)


def body(
    deltas,
    devices,
    n_pts,
    patch_len,
    z_dest,
    x_hbm,
    cells_hbm,
    gain_hbm,
    wqkv_hbm,
    wo_hbm,
    wup_hbm,
    wdown_hbm,
    wpool_hbm,
    out,
    x_ref,
    cells,
    gain,
    wqkv,
    wo,
    wup,
    wdown,
    wpool,
    hs,
    hns,
    sigma,
    spare,
    x_first,
    x_second,
    y_send,
    wq_t,
    wk2,
    kk,
    qt,
    vt,
    ot,
    s_a,
    s_b,
    m_a,
    m_b,
    meta_send,
    meta_recv,
    rim_send,
    rim_recv,
    send_sem,
    recv_sem,
    meta_send_sem,
    meta_recv_sem,
    rim_send_sem,
    rim_recv_sem,
    load_sem,
):
    loads = [
        pltpu.make_async_copy(src, dst, load_sem.at[n])
        for n, (src, dst) in enumerate(
            (
                (x_hbm, x_ref),
                (gain_hbm, gain),
                (wqkv_hbm, wqkv),
                (wo_hbm, wo),
                (wup_hbm, wup),
                (wdown_hbm, wdown),
                (cells_hbm, cells),
                (wpool_hbm, wpool),
            )
        )
    ]
    for load in loads:
        load.start()
    me = lax.axis_index("grp") * n_pts + lax.axis_index("pts")

    def device(delta):
        flat = (me + delta + devices) % devices
        return (flat // n_pts, flat % n_pts)

    barrier = pltpu.get_barrier_semaphore()
    for delta in deltas:
        if delta:
            pl.semaphore_signal(barrier, inc=1, device_id=device(delta), device_id_type=MESH)
    pl.semaphore_wait(barrier, NB - 1)

    def remote(src, dst, ssem, rsem, delta):
        return pltpu.make_async_remote_copy(
            src_ref=src, dst_ref=dst, send_sem=ssem, recv_sem=rsem,
            device_id=device(delta), device_id_type=MESH,
        )

    def block_copy(slot):
        rows = pl.ds(slot * BLK, BLK)
        return remote(
            y_send.at[rows], x_second.at[rows], send_sem.at[slot], recv_sem.at[slot], deltas[slot]
        )

    def meta_copy(slot):
        return remote(
            meta_send.at[slot], meta_recv.at[slot], meta_send_sem.at[slot],
            meta_recv_sem.at[slot], deltas[slot],
        )

    qt[...] = jnp.zeros_like(qt)
    for load in loads[:3]:
        load.wait()
    row = lax.broadcasted_iota(jnp.int32, (8, C), 0)
    for slot, delta in enumerate(deltas):
        base = ((me + delta + devices) % devices) * NB
        block = jnp.int32(0)
        place = jnp.int32(0)
        for n in range(NB):
            offset = z_dest[n] - base
            hit = jnp.logical_and(offset >= 0, offset < NB)
            block = block + jnp.where(hit, n, 0)
            place = place + jnp.where(hit, offset, 0)
        block = jnp.minimum(block, NB - 1)
        x_first[pl.ds(slot * BLK, BLK), :] = x_ref[block]
        limit = patch_len[0] - block * BLK
        meta = jnp.where(row == 1, limit, place)
        meta_send[slot] = meta
        if delta == 0:
            meta_recv[slot] = meta
    for slot, delta in enumerate(deltas):
        if delta:
            meta_copy(slot).start()

    chunks = PATCH // ROWS
    prepare(0, gain, wqkv, wq_t, wk2, sigma)
    for chunk in range(chunks):
        project(0, chunk, x_first, meta_send, gain, wq_t, wk2, kk, qt, vt, spare)
    attention(kk, qt, vt, ot, sigma, spare, s_a, s_b, m_a, m_b)
    for load in loads[3:]:
        load.wait()
    for chunk in range(chunks):
        residual(0, chunk, x_first, gain, ot, wo, hs, hns)
    for chunk in range(chunks):
        y = feed_forward(0, chunk, hs, hns, wup, wdown)
        for part in range(2):
            slot = chunk * 2 + part
            rows = pl.ds(slot * BLK, BLK)
            piece = y[part * BLK : (part + 1) * BLK, :]
            if deltas[slot]:
                y_send[rows, :] = piece
                block_copy(slot).start()
            else:
                x_second[rows, :] = piece

    prepare(1, gain, wqkv, wq_t, wk2, sigma)
    for slot, delta in enumerate(deltas):
        if delta:
            meta_copy(slot).wait()
    for chunk in range(chunks):
        for slot in (chunk * 2, chunk * 2 + 1):
            if deltas[slot]:
                block_copy(slot).wait()
        project(1, chunk, x_second, meta_recv, gain, wq_t, wk2, kk, qt, vt, spare)
    attention(kk, qt, vt, ot, sigma, spare, s_a, s_b, m_a, m_b)
    for chunk in range(chunks):
        residual(1, chunk, x_second, gain, ot, wo, hs, hns)

    number = lax.broadcasted_iota(jnp.int32, (POOL_ROWS, BLK), 0)
    wanted = jnp.where(number == CELL_DEV, -1, jnp.where(number > CELL_DEV, -5, number))
    lane = lax.broadcasted_iota(jnp.int32, (1, BLK), 1)
    ones = jnp.ones((ROWS, 128), bf16)
    sums = jnp.zeros((POOL_ROWS, C), f32)
    counts = jnp.zeros((POOL_ROWS, 128), f32)
    for chunk in range(chunks):
        y = feed_forward(1, chunk, hs, hns, wup, wdown)
        members = []
        for slot in (chunk * 2, chunk * 2 + 1):
            place = meta_recv[slot, 0:1, 0:BLK]
            cell = jnp.zeros((1, BLK), jnp.int32)
            for n in range(NB):
                cell = cell + jnp.where(place == n, cells[n : n + 1, :], 0)
            cell = jnp.where(lane < meta_recv[slot, 1:2, 0:BLK], cell - me * CELL_DEV, -9)
            members.append((cell == wanted).astype(f32).astype(bf16))
        member = jnp.concatenate(members, axis=1)
        sums = sums + dot(member, y)
        counts = counts + dot(member, ones)

    rim_send[:, 0:C] = sums[CELL_DEV : CELL_DEV + 8, :]
    rim_send[:, C : C + 128] = counts[CELL_DEV : CELL_DEV + 8, :]
    rim = remote(rim_send, rim_recv, rim_send_sem, rim_recv_sem, -1)
    rim.start()

    def pooled(total, count):
        count = jnp.maximum(count, 1.0)
        mean = total / jnp.concatenate([count, count], axis=1)
        return gelu(dot(mean.astype(bf16), wpool[...])).astype(bf16)

    out[...] = pooled(sums[:CELL_DEV, :], counts[:CELL_DEV, :])
    rim.wait()
    tail = CELL_DEV - 16
    last = lax.broadcasted_iota(jnp.int32, (16, 1), 0) == 15
    extra = jnp.where(last, rim_recv[0:1, 0:C], 0.0)
    extra_count = jnp.where(last, rim_recv[0:1, C : C + 128], 0.0)
    out[tail:, :] = pooled(
        sums[tail:CELL_DEV, :] + extra, counts[tail:CELL_DEV, :] + extra_count
    )


def on_device(
    points_z,
    patch_len,
    z_dest,
    cell_of,
    norm_gain,
    qkv_weight,
    out_weight,
    up_weight,
    down_weight,
    pool_weight,
):
    n_pts = lax.axis_size("pts")
    devices = lax.axis_size(("grp", "pts"))
    deltas = (3, -3, 2, -2, 1, -1, devices // 2, 0)
    vmem = pl.BlockSpec(memory_space=pltpu.VMEM)
    smem = pl.BlockSpec(memory_space=pltpu.SMEM)
    return pl.pallas_call(
        functools.partial(body, deltas, devices, n_pts),
        out_shape=jax.ShapeDtypeStruct((CELL_DEV, CP), bf16),
        in_specs=[smem, smem] + [pl.BlockSpec(memory_space=pl.ANY)] * 8,
        out_specs=vmem,
        scratch_shapes=[
            pltpu.VMEM((NB, BLK, C), bf16),
            pltpu.VMEM((NB, BLK), jnp.int32),
            pltpu.VMEM((2, 2, C), f32),
            pltpu.VMEM((2, C, 3 * C), bf16),
            pltpu.VMEM((2, C, C), bf16),
            pltpu.VMEM((2, C, FF), bf16),
            pltpu.VMEM((2, FF, C), bf16),
            pltpu.VMEM((C, CP), bf16),
            pltpu.VMEM((PATCH, C), bf16),
            pltpu.VMEM((PATCH, C), bf16),
            pltpu.VMEM((HEADS, 8, QW), f32),
            pltpu.VMEM((NB, QW), f32),
            pltpu.VMEM((PATCH, C), bf16),
            pltpu.VMEM((PATCH, C), bf16),
            pltpu.VMEM((PATCH, C), bf16),
            pltpu.VMEM((2 * C, C), bf16),
            pltpu.VMEM((C, 2 * C), bf16),
            pltpu.VMEM((4, PATCH, 128), f8),
            pltpu.VMEM((HEADS, C, PATCH), f8),
            pltpu.VMEM((HEADS, HD, PATCH), bf16),
            pltpu.VMEM((C, PATCH), bf16),
            pltpu.VMEM((PATCH, QW), f32),
            pltpu.VMEM((PATCH, QW), f32),
            pltpu.VMEM((8, QW), f32),
            pltpu.VMEM((8, QW), f32),
            pltpu.VMEM((NB, 8, C), jnp.int32),
            pltpu.VMEM((NB, 8, C), jnp.int32),
            pltpu.VMEM((8, C + 128), f32),
            pltpu.VMEM((8, C + 128), f32),
            pltpu.SemaphoreType.DMA((NB,)),
            pltpu.SemaphoreType.DMA((NB,)),
            pltpu.SemaphoreType.DMA((NB,)),
            pltpu.SemaphoreType.DMA((NB,)),
            pltpu.SemaphoreType.DMA,
            pltpu.SemaphoreType.DMA,
            pltpu.SemaphoreType.DMA((8,)),
        ],
        compiler_params=pltpu.CompilerParams(
            collective_id=0, has_side_effects=True, vmem_limit_bytes=60 * 2**20
        ),
        name="encoder",
    )(
        patch_len,
        z_dest,
        points_z.reshape(NB, BLK, C),
        cell_of.reshape(NB, BLK),
        norm_gain,
        qkv_weight,
        out_weight,
        up_weight,
        down_weight,
        pool_weight,
    )


def solution(mesh):
    placed = (
        P(("grp", "pts"), None),
        P(("grp", "pts")),
        P(("grp", "pts")),
        P(("grp", "pts")),
        P(),
        P(),
        P(),
        P(),
        P(),
        P(),
    )
    return jax.shard_map(
        on_device, mesh=mesh, in_specs=placed, out_specs=P(("grp", "pts"), None), check_vma=False
    )
```

```python
import functools

import jax
import jax.numpy as jnp
from jax import lax
from jax.experimental import pallas as pl
from jax.experimental.pallas import tpu as pltpu
from jax.sharding import PartitionSpec as P

C = 256
HEADS = 16
HD = 16
PATCH = 1024
BLK = 128
NB = 8
CELL_DEV = 256
CP = 512
FF = 1024
NORM_EPS = 1e-05
QW = 512
TILES = PATCH // QW
ROWS = 256
LOG2E = 1.4426950408889634
POOL_ROWS = 272
ERF = (
    0.7978281360364785,
    0.03646879080750627,
    -0.00012486153426078468,
    -3.0581026877848916e-05,
    1.1190833948473977e-06,
)
F8_TOP = 400.0
bf16 = jnp.bfloat16
f8 = jnp.float8_e4m3fn
f32 = jnp.float32
MESH = pl.DeviceIdType.MESH


def gelu(x):
    u = x * x
    r = ERF[4]
    for coefficient in ERF[3::-1]:
        r = r * u + coefficient
    half = 0.5 * x
    return half + half * jnp.tanh(x * r)


def norm(x, gain):
    centered = x - jnp.mean(x, axis=-1, keepdims=True)
    variance = jnp.mean(centered * centered, axis=-1, keepdims=True)
    return (centered * lax.rsqrt(variance + NORM_EPS) * gain).astype(bf16)


def dot(a, b):
    return jnp.dot(a, b, preferred_element_type=f32)


def dot_nt(a, b):
    return lax.dot_general(a, b, (((1,), (1,)), ((), ())), preferred_element_type=f32)


def dot_tn(a, b):
    return lax.dot_general(a, b, (((0,), (0,)), ((), ())), preferred_element_type=f32)


def prepare(b, gain, wqkv, wq_t, wk2, sigma):
    reach = 16.1 * jnp.max(jnp.abs(gain[b, 0:1, :]))
    column = lax.broadcasted_iota(jnp.int32, (C, C), 0) // HD
    same_head = (column == lax.broadcasted_iota(jnp.int32, (C, C), 1) // HD).astype(f32).astype(bf16)

    def power(exponent):
        return jnp.exp2(exponent).astype(bf16).astype(f32)

    def exponents(w):
        squares = jnp.sum(w * w, axis=0, keepdims=True)
        squares = jnp.broadcast_to(squares, (16, C)).astype(bf16)
        total = jnp.maximum(dot(squares, same_head)[0:1, :], 1e-30)
        bound = reach * jnp.sqrt(total)
        return jnp.floor(jnp.log(F8_TOP / bound) * LOG2E)

    wq = wqkv[b, :, 0:C].astype(f32)
    wk = wqkv[b, :, C : 2 * C].astype(f32)
    wv = wqkv[b, :, 2 * C : 3 * C].astype(f32)
    q_up, k_up = exponents(wq), exponents(wk)
    wq_t[0:C, :] = (wq * power(q_up)).T.astype(bf16)
    wq_t[C : 2 * C, :] = wv.T.astype(bf16)
    column = lax.broadcasted_iota(jnp.int32, (C, 2 * C), 0)
    wide = lax.broadcasted_iota(jnp.int32, (C, 2 * C), 1)
    twice = (column == (wide // (2 * HD)) * HD + wide % HD).astype(f32).astype(bf16)
    wk2[...] = dot((wk * power(k_up)).astype(bf16), twice).astype(bf16)
    back = power(-q_up - k_up) * (HD**-0.5 * LOG2E)
    for h in range(HEADS):
        sigma[h] = jnp.broadcast_to(back[:, h * HD : h * HD + 1], (8, QW))


def project(b, chunk, xs, meta, gain, wq_t, wk2, kk, qt, vt):
    rows = pl.ds(chunk * ROWS, ROWS)
    xn = norm(xs[rows, :].astype(f32), gain[b, 0:1, :])
    k = dot(xn, wk2[...]).astype(bf16).astype(f32)
    is_high = lax.broadcasted_iota(jnp.int32, (BLK, 2 * C), 1) % (2 * HD) < HD
    for part in range(2):
        slot = chunk * 2 + part
        limit = meta[slot, 1:2, :]
        limit = jnp.concatenate([limit, limit], axis=1)
        live = lax.broadcasted_iota(jnp.int32, (BLK, 2 * C), 0) < limit
        piece = k[part * BLK : (part + 1) * BLK, :]
        piece = jnp.where(live, piece, piece[0:1, :])
        high = piece.astype(f8).astype(f32)
        piece = jnp.where(is_high, high, piece - high).astype(f8)
        for g in range(4):
            kk[g, pl.ds(slot * BLK, BLK), :] = piece[:, g * 128 : (g + 1) * 128]
    qv = dot_nt(wq_t[...], xn)
    q = qv[:C, :].astype(bf16).astype(f32)
    high = q.astype(f8).astype(f32)
    low = q - high
    for h in range(HEADS):
        r = (h % 4) * 2 * HD
        at = slice(h * HD, (h + 1) * HD)
        qt[h, r : r + 2 * HD, rows] = jnp.concatenate([high[at], high[at]], axis=0).astype(f8)
        qt[h, 128 + r : 128 + r + 2 * HD, rows] = jnp.concatenate(
            [low[at], low[at]], axis=0
        ).astype(f8)
    limits = jnp.concatenate(
        [meta[chunk * 2, 1:2, 0:BLK], meta[chunk * 2 + 1, 1:2, 0:BLK]], axis=1
    )
    lane = lax.broadcasted_iota(jnp.int32, (1, ROWS), 1) % BLK
    live_row = (lane < limits).astype(f32)
    v = (qv[C:, :] * live_row).astype(bf16)
    first = lax.broadcasted_iota(jnp.int32, (HD, ROWS), 0) == 0
    ones = jnp.where(first, live_row, 0.0).astype(bf16)
    for h in range(HEADS):
        vt[h, 0:HD, rows] = v[h * HD : (h + 1) * HD, :]
        vt[h, HD : 2 * HD, rows] = ones


def scores(step, kk, qt, sigma, s, m):
    h, t = step % HEADS, step // HEADS
    keys = kk[h // 4]
    queries = qt[h, :, pl.ds(pl.multiple_of(t * QW, QW), QW)]
    raw = dot(jnp.concatenate([keys, keys], axis=1), queries) * sigma[h][0:1, :]
    s[...] = raw
    m[...] = jnp.max(raw.reshape(PATCH // 8, 8, QW), axis=0)


def values(h, t, vt, ot, s, m):
    top = jnp.max(m[...], axis=0, keepdims=True)
    total = None
    for c in range(PATCH // 256):
        keys = pl.ds(c * 256, 256)
        e = jnp.exp2(s[keys, :] - top).astype(bf16)
        part = dot(vt[h, :, keys], e)
        total = part if total is None else total + part
    ot[pl.ds(pl.multiple_of(h * HD, HD), HD), pl.ds(t * QW, QW)] = (
        total[0:HD, :] / total[HD : HD + 1, :]
    ).astype(bf16)


def attention(t, kk, qt, vt, ot, sigma, s_a, s_b, m_a, m_b):
    if t == 0:
        scores(0, kk, qt, sigma, s_a, m_a)

    def pair(n, carry):
        h = 2 * n
        step = t * HEADS + h
        scores(step + 1, kk, qt, sigma, s_b, m_b)
        values(h, t, vt, ot, s_a, m_a)
        scores(jnp.minimum(step + 2, TILES * HEADS - 1), kk, qt, sigma, s_a, m_a)
        values(h + 1, t, vt, ot, s_b, m_b)
        return carry

    lax.fori_loop(0, HEADS // 2, pair, 0)


def residual(b, chunk, xs, gain, ot, wo, hs, hns):
    rows = pl.ds(chunk * ROWS, ROWS)
    h = (xs[rows, :].astype(f32) + dot_tn(ot[:, rows], wo[b])).astype(bf16)
    hs[rows, :] = h
    hns[rows, :] = norm(h.astype(f32), gain[b, 1:2, :])


def feed_forward(b, chunk, hs, hns, wup, wdown):
    rows = pl.ds(chunk * ROWS, ROWS)
    u = gelu(dot(hns[rows, :], wup[b])).astype(bf16)
    return (hs[rows, :].astype(f32) + dot(u, wdown[b])).astype(bf16)


def body(
    deltas,
    devices,
    n_pts,
    patch_len,
    z_dest,
    x_hbm,
    cells_hbm,
    gain_hbm,
    wqkv_hbm,
    wo_hbm,
    wup_hbm,
    wdown_hbm,
    wpool_hbm,
    out,
    x_ref,
    cells,
    gain,
    wqkv,
    wo,
    wup,
    wdown,
    wpool,
    hs,
    hns,
    sigma,
    x_first,
    x_second,
    y_send,
    wq_t,
    wk2,
    kk,
    qt,
    vt,
    ot,
    s_a,
    s_b,
    m_a,
    m_b,
    meta_send,
    meta_recv,
    rim_send,
    rim_recv,
    send_sem,
    recv_sem,
    meta_send_sem,
    meta_recv_sem,
    rim_send_sem,
    rim_recv_sem,
    load_sem,
):
    loads = [
        pltpu.make_async_copy(src, dst, load_sem.at[n])
        for n, (src, dst) in enumerate(
            (
                (x_hbm, x_ref),
                (gain_hbm, gain),
                (wqkv_hbm, wqkv),
                (wo_hbm, wo),
                (wup_hbm, wup),
                (wdown_hbm, wdown),
                (cells_hbm, cells),
                (wpool_hbm, wpool),
            )
        )
    ]
    for load in loads:
        load.start()
    me = lax.axis_index("grp") * n_pts + lax.axis_index("pts")

    def device(delta):
        flat = (me + delta + devices) % devices
        return (flat // n_pts, flat % n_pts)

    barrier = pltpu.get_barrier_semaphore()
    for delta in deltas:
        if delta:
            pl.semaphore_signal(barrier, inc=1, device_id=device(delta), device_id_type=MESH)

    def remote(src, dst, ssem, rsem, delta):
        return pltpu.make_async_remote_copy(
            src_ref=src, dst_ref=dst, send_sem=ssem, recv_sem=rsem,
            device_id=device(delta), device_id_type=MESH,
        )

    def block_copy(slot):
        rows = pl.ds(slot * BLK, BLK)
        return remote(
            y_send.at[rows], x_second.at[rows], send_sem.at[slot], recv_sem.at[slot], deltas[slot]
        )

    def meta_copy(slot):
        return remote(
            meta_send.at[slot], meta_recv.at[slot], meta_send_sem.at[slot],
            meta_recv_sem.at[slot], deltas[slot],
        )

    qt[...] = jnp.zeros_like(qt)
    for load in loads[:3]:
        load.wait()
    row = lax.broadcasted_iota(jnp.int32, (8, C), 0)
    for slot, delta in enumerate(deltas):
        base = ((me + delta + devices) % devices) * NB
        block = jnp.int32(0)
        place = jnp.int32(0)
        for n in range(NB):
            offset = z_dest[n] - base
            hit = jnp.logical_and(offset >= 0, offset < NB)
            block = block + jnp.where(hit, n, 0)
            place = place + jnp.where(hit, offset, 0)
        block = jnp.minimum(block, NB - 1)
        x_first[pl.ds(slot * BLK, BLK), :] = x_ref[block]
        limit = patch_len[0] - block * BLK
        meta = jnp.where(row == 1, limit, place)
        meta_send[slot] = meta
        if delta == 0:
            meta_recv[slot] = meta
    chunks = PATCH // ROWS
    prepare(0, gain, wqkv, wq_t, wk2, sigma)
    for chunk in range(chunks):
        project(0, chunk, x_first, meta_send, gain, wq_t, wk2, kk, qt, vt)
    pl.semaphore_wait(barrier, NB - 1)
    for slot, delta in enumerate(deltas):
        if delta:
            meta_copy(slot).start()
    per_tile = chunks // TILES
    for t in range(TILES):
        attention(t, kk, qt, vt, ot, sigma, s_a, s_b, m_a, m_b)
        if t == 0:
            for load in loads[3:]:
                load.wait()
        mine = range(t * per_tile, (t + 1) * per_tile)
        for chunk in mine:
            residual(0, chunk, x_first, gain, ot, wo, hs, hns)
        for chunk in mine:
            y = feed_forward(0, chunk, hs, hns, wup, wdown)
            for part in range(2):
                slot = chunk * 2 + part
                rows = pl.ds(slot * BLK, BLK)
                piece = y[part * BLK : (part + 1) * BLK, :]
                if deltas[slot]:
                    y_send[rows, :] = piece
                    block_copy(slot).start()
                else:
                    x_second[rows, :] = piece

    prepare(1, gain, wqkv, wq_t, wk2, sigma)
    for slot, delta in enumerate(deltas):
        if delta:
            meta_copy(slot).wait()
    for chunk in range(chunks):
        for slot in (chunk * 2, chunk * 2 + 1):
            if deltas[slot]:
                block_copy(slot).wait()
        project(1, chunk, x_second, meta_recv, gain, wq_t, wk2, kk, qt, vt)
    for t in range(TILES):
        attention(t, kk, qt, vt, ot, sigma, s_a, s_b, m_a, m_b)
    for chunk in range(chunks):
        residual(1, chunk, x_second, gain, ot, wo, hs, hns)

    number = lax.broadcasted_iota(jnp.int32, (POOL_ROWS, BLK), 0)
    wanted = jnp.where(number == CELL_DEV, -1, jnp.where(number > CELL_DEV, -5, number))
    lane = lax.broadcasted_iota(jnp.int32, (1, BLK), 1)
    ones = jnp.ones((ROWS, 128), bf16)
    sums = jnp.zeros((POOL_ROWS, C), f32)
    counts = jnp.zeros((POOL_ROWS, 128), f32)
    for chunk in range(chunks):
        y = feed_forward(1, chunk, hs, hns, wup, wdown)
        members = []
        for slot in (chunk * 2, chunk * 2 + 1):
            place = meta_recv[slot, 0:1, 0:BLK]
            cell = jnp.zeros((1, BLK), jnp.int32)
            for n in range(NB):
                cell = cell + jnp.where(place == n, cells[n : n + 1, :], 0)
            cell = jnp.where(lane < meta_recv[slot, 1:2, 0:BLK], cell - me * CELL_DEV, -9)
            members.append((cell == wanted).astype(f32).astype(bf16))
        member = jnp.concatenate(members, axis=1)
        sums = sums + dot(member, y)
        counts = counts + dot(member, ones)

    rim_send[:, 0:C] = sums[CELL_DEV : CELL_DEV + 8, :]
    rim_send[:, C : C + 128] = counts[CELL_DEV : CELL_DEV + 8, :]
    rim = remote(rim_send, rim_recv, rim_send_sem, rim_recv_sem, -1)
    rim.start()

    def pooled(total, count):
        count = jnp.maximum(count, 1.0)
        mean = total / jnp.concatenate([count, count], axis=1)
        return gelu(dot(mean.astype(bf16), wpool[...])).astype(bf16)

    out[...] = pooled(sums[:CELL_DEV, :], counts[:CELL_DEV, :])
    rim.wait()
    tail = CELL_DEV - 16
    last = lax.broadcasted_iota(jnp.int32, (16, 1), 0) == 15
    extra = jnp.where(last, rim_recv[0:1, 0:C], 0.0)
    extra_count = jnp.where(last, rim_recv[0:1, C : C + 128], 0.0)
    out[tail:, :] = pooled(
        sums[tail:CELL_DEV, :] + extra, counts[tail:CELL_DEV, :] + extra_count
    )


def on_device(
    points_z,
    patch_len,
    z_dest,
    cell_of,
    norm_gain,
    qkv_weight,
    out_weight,
    up_weight,
    down_weight,
    pool_weight,
):
    n_pts = lax.axis_size("pts")
    devices = lax.axis_size(("grp", "pts"))
    deltas = (3, -3, 2, -2, 1, -1, devices // 2, 0)
    vmem = pl.BlockSpec(memory_space=pltpu.VMEM)
    smem = pl.BlockSpec(memory_space=pltpu.SMEM)
    return pl.pallas_call(
        functools.partial(body, deltas, devices, n_pts),
        out_shape=jax.ShapeDtypeStruct((CELL_DEV, CP), bf16),
        in_specs=[smem, smem] + [pl.BlockSpec(memory_space=pl.ANY)] * 8,
        out_specs=vmem,
        scratch_shapes=[
            pltpu.VMEM((NB, BLK, C), bf16),
            pltpu.VMEM((NB, BLK), jnp.int32),
            pltpu.VMEM((2, 2, C), f32),
            pltpu.VMEM((2, C, 3 * C), bf16),
            pltpu.VMEM((2, C, C), bf16),
            pltpu.VMEM((2, C, FF), bf16),
            pltpu.VMEM((2, FF, C), bf16),
            pltpu.VMEM((C, CP), bf16),
            pltpu.VMEM((PATCH, C), bf16),
            pltpu.VMEM((PATCH, C), bf16),
            pltpu.VMEM((HEADS, 8, QW), f32),
            pltpu.VMEM((PATCH, C), bf16),
            pltpu.VMEM((PATCH, C), bf16),
            pltpu.VMEM((PATCH, C), bf16),
            pltpu.VMEM((2 * C, C), bf16),
            pltpu.VMEM((C, 2 * C), bf16),
            pltpu.VMEM((4, PATCH, 128), f8),
            pltpu.VMEM((HEADS, C, PATCH), f8),
            pltpu.VMEM((HEADS, 2 * HD, PATCH), bf16),
            pltpu.VMEM((C, PATCH), bf16),
            pltpu.VMEM((PATCH, QW), f32),
            pltpu.VMEM((PATCH, QW), f32),
            pltpu.VMEM((8, QW), f32),
            pltpu.VMEM((8, QW), f32),
            pltpu.VMEM((NB, 8, C), jnp.int32),
            pltpu.VMEM((NB, 8, C), jnp.int32),
            pltpu.VMEM((8, C + 128), f32),
            pltpu.VMEM((8, C + 128), f32),
            pltpu.SemaphoreType.DMA((NB,)),
            pltpu.SemaphoreType.DMA((NB,)),
            pltpu.SemaphoreType.DMA((NB,)),
            pltpu.SemaphoreType.DMA((NB,)),
            pltpu.SemaphoreType.DMA,
            pltpu.SemaphoreType.DMA,
            pltpu.SemaphoreType.DMA((8,)),
        ],
        compiler_params=pltpu.CompilerParams(
            collective_id=0, has_side_effects=True, vmem_limit_bytes=60 * 2**20
        ),
        name="encoder",
    )(
        patch_len,
        z_dest,
        points_z.reshape(NB, BLK, C),
        cell_of.reshape(NB, BLK),
        norm_gain,
        qkv_weight,
        out_weight,
        up_weight,
        down_weight,
        pool_weight,
    )


def solution(mesh):
    placed = (
        P(("grp", "pts"), None),
        P(("grp", "pts")),
        P(("grp", "pts")),
        P(("grp", "pts")),
        P(),
        P(),
        P(),
        P(),
        P(),
        P(),
    )
    return jax.shard_map(
        on_device, mesh=mesh, in_specs=placed, out_specs=P(("grp", "pts"), None), check_vma=False
    )
```

```python
import functools

import jax
import jax.numpy as jnp
from jax import lax
from jax.experimental import pallas as pl
from jax.experimental.pallas import tpu as pltpu
from jax.sharding import PartitionSpec as P

C = 256
HEADS = 16
HD = 16
PATCH = 1024
BLK = 128
NB = 8
CELL_DEV = 256
CP = 512
FF = 1024
NORM_EPS = 1e-05
QW = 512
TILES = PATCH // QW
UNROLL = 8
ROWS = 256
LOG2E = 1.4426950408889634
POOL_ROWS = 272
ERF = (
    0.7978281360364785,
    0.03646879080750627,
    -0.00012486153426078468,
    -3.0581026877848916e-05,
    1.1190833948473977e-06,
)
F8_TOP = 400.0
bf16 = jnp.bfloat16
f8 = jnp.float8_e4m3fn
f32 = jnp.float32
MESH = pl.DeviceIdType.MESH


def gelu(x):
    u = x * x
    r = ERF[4]
    for coefficient in ERF[3::-1]:
        r = r * u + coefficient
    half = 0.5 * x
    return half + half * jnp.tanh(x * r)


def norm(x, gain):
    centered = x - jnp.mean(x, axis=-1, keepdims=True)
    variance = jnp.mean(centered * centered, axis=-1, keepdims=True)
    return (centered * lax.rsqrt(variance + NORM_EPS) * gain).astype(bf16)


def dot(a, b):
    return jnp.dot(a, b, preferred_element_type=f32)


def dot_nt(a, b):
    return lax.dot_general(a, b, (((1,), (1,)), ((), ())), preferred_element_type=f32)


def dot_tn(a, b):
    return lax.dot_general(a, b, (((0,), (0,)), ((), ())), preferred_element_type=f32)


def prepare(b, gain, wqkv, wq_t, wk2, sigma):
    reach = 16.1 * jnp.max(jnp.abs(gain[b, 0:1, :]))
    column = lax.broadcasted_iota(jnp.int32, (C, C), 0) // HD
    same_head = (column == lax.broadcasted_iota(jnp.int32, (C, C), 1) // HD).astype(f32).astype(bf16)

    def power(exponent):
        return jnp.exp2(exponent).astype(bf16).astype(f32)

    def exponents(w):
        squares = jnp.sum(w * w, axis=0, keepdims=True)
        squares = jnp.broadcast_to(squares, (16, C)).astype(bf16)
        total = jnp.maximum(dot(squares, same_head)[0:1, :], 1e-30)
        bound = reach * jnp.sqrt(total)
        return jnp.floor(jnp.log(F8_TOP / bound) * LOG2E)

    wq = wqkv[b, :, 0:C].astype(f32)
    wk = wqkv[b, :, C : 2 * C].astype(f32)
    wv = wqkv[b, :, 2 * C : 3 * C].astype(f32)
    q_up, k_up = exponents(wq), exponents(wk)
    wq_t[0:C, :] = (wq * power(q_up)).T.astype(bf16)
    wq_t[C : 2 * C, :] = wv.T.astype(bf16)
    column = lax.broadcasted_iota(jnp.int32, (C, 2 * C), 0)
    wide = lax.broadcasted_iota(jnp.int32, (C, 2 * C), 1)
    twice = (column == (wide // (2 * HD)) * HD + wide % HD).astype(f32).astype(bf16)
    wk2[...] = dot((wk * power(k_up)).astype(bf16), twice).astype(bf16)
    back = power(-q_up - k_up) * (HD**-0.5 * LOG2E)
    for h in range(HEADS):
        sigma[h] = jnp.broadcast_to(back[:, h * HD : h * HD + 1], (8, QW))


def project(b, chunk, xs, meta, gain, wq_t, wk2, kk, qt, vt):
    rows = pl.ds(chunk * ROWS, ROWS)
    xn = norm(xs[rows, :].astype(f32), gain[b, 0:1, :])
    k = dot(xn, wk2[...]).astype(bf16).astype(f32)
    is_high = lax.broadcasted_iota(jnp.int32, (BLK, 2 * C), 1) % (2 * HD) < HD
    for part in range(2):
        slot = chunk * 2 + part
        limit = meta[slot, 1:2, :]
        limit = jnp.concatenate([limit, limit], axis=1)
        live = lax.broadcasted_iota(jnp.int32, (BLK, 2 * C), 0) < limit
        piece = k[part * BLK : (part + 1) * BLK, :]
        piece = jnp.where(live, piece, piece[0:1, :])
        high = piece.astype(f8).astype(f32)
        piece = jnp.where(is_high, high, piece - high).astype(f8)
        for g in range(4):
            kk[g, pl.ds(slot * BLK, BLK), :] = piece[:, g * 128 : (g + 1) * 128]
    qv = dot_nt(wq_t[...], xn)
    q = qv[:C, :].astype(bf16).astype(f32)
    high = q.astype(f8).astype(f32)
    low = q - high
    for h in range(HEADS):
        r = (h % 4) * 2 * HD
        at = slice(h * HD, (h + 1) * HD)
        qt[h, r : r + 2 * HD, rows] = jnp.concatenate([high[at], high[at]], axis=0).astype(f8)
        qt[h, 128 + r : 128 + r + 2 * HD, rows] = jnp.concatenate(
            [low[at], low[at]], axis=0
        ).astype(f8)
    limits = jnp.concatenate(
        [meta[chunk * 2, 1:2, 0:BLK], meta[chunk * 2 + 1, 1:2, 0:BLK]], axis=1
    )
    lane = lax.broadcasted_iota(jnp.int32, (1, ROWS), 1) % BLK
    live_row = (lane < limits).astype(f32)
    v = (qv[C:, :] * live_row).astype(bf16)
    first = lax.broadcasted_iota(jnp.int32, (HD, ROWS), 0) == 0
    ones = jnp.where(first, live_row, 0.0).astype(bf16)
    for h in range(HEADS):
        vt[h, 0:HD, rows] = v[h * HD : (h + 1) * HD, :]
        vt[h, HD : 2 * HD, rows] = ones


def scores(step, kk, qt, sigma, s, m):
    h, t = step % HEADS, step // HEADS
    keys = kk[h // 4]
    queries = qt[h, :, pl.ds(pl.multiple_of(t * QW, QW), QW)]
    raw = dot(jnp.concatenate([keys, keys], axis=1), queries) * sigma[h][0:1, :]
    s[...] = raw
    m[...] = jnp.max(raw.reshape(PATCH // 8, 8, QW), axis=0)


def values(h, t, vt, ot, s, m):
    top = jnp.max(m[...], axis=0, keepdims=True)
    total = None
    for c in range(PATCH // 256):
        keys = pl.ds(c * 256, 256)
        e = jnp.exp2(s[keys, :] - top).astype(bf16)
        part = dot(vt[h, :, keys], e)
        total = part if total is None else total + part
    ot[pl.ds(pl.multiple_of(h * HD, HD), HD), pl.ds(t * QW, QW)] = (
        total[0:HD, :] / total[HD : HD + 1, :]
    ).astype(bf16)


def attention(t, kk, qt, vt, ot, sigma, s_a, s_b, m_a, m_b):
    if t == 0:
        scores(0, kk, qt, sigma, s_a, m_a)

    def group(n, carry):
        for o in range(0, UNROLL, 2):
            h = UNROLL * n + o
            step = t * HEADS + h
            scores(step + 1, kk, qt, sigma, s_b, m_b)
            values(h, t, vt, ot, s_a, m_a)
            scores(jnp.minimum(step + 2, TILES * HEADS - 1), kk, qt, sigma, s_a, m_a)
            values(h + 1, t, vt, ot, s_b, m_b)
        return carry

    lax.fori_loop(0, HEADS // UNROLL, group, 0)


def residual(b, chunk, xs, gain, ot, wo, hs, hns):
    rows = pl.ds(chunk * ROWS, ROWS)
    h = (xs[rows, :].astype(f32) + dot_tn(ot[:, rows], wo[b])).astype(bf16)
    hs[rows, :] = h
    hns[rows, :] = norm(h.astype(f32), gain[b, 1:2, :])


def feed_forward(b, chunk, hs, hns, wup, wdown):
    rows = pl.ds(chunk * ROWS, ROWS)
    u = gelu(dot(hns[rows, :], wup[b])).astype(bf16)
    return (hs[rows, :].astype(f32) + dot(u, wdown[b])).astype(bf16)


def body(
    deltas,
    devices,
    n_pts,
    patch_len,
    z_dest,
    x_hbm,
    cells_hbm,
    gain_hbm,
    wqkv_hbm,
    wo_hbm,
    wup_hbm,
    wdown_hbm,
    wpool_hbm,
    out,
    x_ref,
    cells,
    gain,
    wqkv,
    wo,
    wup,
    wdown,
    wpool,
    hs,
    hns,
    sigma,
    x_first,
    x_second,
    y_send,
    wq_t,
    wk2,
    kk,
    qt,
    vt,
    ot,
    s_a,
    s_b,
    m_a,
    m_b,
    meta_send,
    meta_recv,
    rim_send,
    rim_recv,
    send_sem,
    recv_sem,
    meta_send_sem,
    meta_recv_sem,
    rim_send_sem,
    rim_recv_sem,
    load_sem,
):
    loads = [
        pltpu.make_async_copy(src, dst, load_sem.at[n])
        for n, (src, dst) in enumerate(
            (
                (x_hbm, x_ref),
                (gain_hbm, gain),
                (wqkv_hbm, wqkv),
                (wo_hbm, wo),
                (wup_hbm, wup),
                (wdown_hbm, wdown),
                (cells_hbm, cells),
                (wpool_hbm, wpool),
            )
        )
    ]
    for load in loads:
        load.start()
    me = lax.axis_index("grp") * n_pts + lax.axis_index("pts")

    def device(delta):
        flat = (me + delta + devices) % devices
        return (flat // n_pts, flat % n_pts)

    barrier = pltpu.get_barrier_semaphore()
    for delta in deltas:
        if delta:
            pl.semaphore_signal(barrier, inc=1, device_id=device(delta), device_id_type=MESH)

    def remote(src, dst, ssem, rsem, delta):
        return pltpu.make_async_remote_copy(
            src_ref=src, dst_ref=dst, send_sem=ssem, recv_sem=rsem,
            device_id=device(delta), device_id_type=MESH,
        )

    def block_copy(slot):
        rows = pl.ds(slot * BLK, BLK)
        return remote(
            y_send.at[rows], x_second.at[rows], send_sem.at[slot], recv_sem.at[slot], deltas[slot]
        )

    def meta_copy(slot):
        return remote(
            meta_send.at[slot], meta_recv.at[slot], meta_send_sem.at[slot],
            meta_recv_sem.at[slot], deltas[slot],
        )

    qt[...] = jnp.zeros_like(qt)
    for load in loads[:3]:
        load.wait()
    row = lax.broadcasted_iota(jnp.int32, (8, C), 0)
    for slot, delta in enumerate(deltas):
        base = ((me + delta + devices) % devices) * NB
        block = jnp.int32(0)
        place = jnp.int32(0)
        for n in range(NB):
            offset = z_dest[n] - base
            hit = jnp.logical_and(offset >= 0, offset < NB)
            block = block + jnp.where(hit, n, 0)
            place = place + jnp.where(hit, offset, 0)
        block = jnp.minimum(block, NB - 1)
        x_first[pl.ds(slot * BLK, BLK), :] = x_ref[block]
        limit = patch_len[0] - block * BLK
        meta = jnp.where(row == 1, limit, place)
        meta_send[slot] = meta
        if delta == 0:
            meta_recv[slot] = meta
    chunks = PATCH // ROWS
    prepare(0, gain, wqkv, wq_t, wk2, sigma)
    for chunk in range(chunks):
        project(0, chunk, x_first, meta_send, gain, wq_t, wk2, kk, qt, vt)
    pl.semaphore_wait(barrier, NB - 1)
    for slot, delta in enumerate(deltas):
        if delta:
            meta_copy(slot).start()
    per_tile = chunks // TILES
    for t in range(TILES):
        attention(t, kk, qt, vt, ot, sigma, s_a, s_b, m_a, m_b)
        if t == 0:
            for load in loads[3:]:
                load.wait()
        mine = range(t * per_tile, (t + 1) * per_tile)
        for chunk in mine:
            residual(0, chunk, x_first, gain, ot, wo, hs, hns)
        for chunk in mine:
            y = feed_forward(0, chunk, hs, hns, wup, wdown)
            for part in range(2):
                slot = chunk * 2 + part
                rows = pl.ds(slot * BLK, BLK)
                piece = y[part * BLK : (part + 1) * BLK, :]
                if deltas[slot]:
                    y_send[rows, :] = piece
                    block_copy(slot).start()
                else:
                    x_second[rows, :] = piece

    prepare(1, gain, wqkv, wq_t, wk2, sigma)
    for slot, delta in enumerate(deltas):
        if delta:
            meta_copy(slot).wait()
    for chunk in range(chunks):
        for slot in (chunk * 2, chunk * 2 + 1):
            if deltas[slot]:
                block_copy(slot).wait()
        project(1, chunk, x_second, meta_recv, gain, wq_t, wk2, kk, qt, vt)
    for t in range(TILES):
        attention(t, kk, qt, vt, ot, sigma, s_a, s_b, m_a, m_b)
    for chunk in range(chunks):
        residual(1, chunk, x_second, gain, ot, wo, hs, hns)

    number = lax.broadcasted_iota(jnp.int32, (POOL_ROWS, BLK), 0)
    wanted = jnp.where(number == CELL_DEV, -1, jnp.where(number > CELL_DEV, -5, number))
    lane = lax.broadcasted_iota(jnp.int32, (1, BLK), 1)
    ones = jnp.ones((ROWS, 128), bf16)
    sums = jnp.zeros((POOL_ROWS, C), f32)
    counts = jnp.zeros((POOL_ROWS, 128), f32)
    for chunk in range(chunks):
        y = feed_forward(1, chunk, hs, hns, wup, wdown)
        members = []
        for slot in (chunk * 2, chunk * 2 + 1):
            place = meta_recv[slot, 0:1, 0:BLK]
            cell = jnp.zeros((1, BLK), jnp.int32)
            for n in range(NB):
                cell = cell + jnp.where(place == n, cells[n : n + 1, :], 0)
            cell = jnp.where(lane < meta_recv[slot, 1:2, 0:BLK], cell - me * CELL_DEV, -9)
            members.append((cell == wanted).astype(f32).astype(bf16))
        member = jnp.concatenate(members, axis=1)
        sums = sums + dot(member, y)
        counts = counts + dot(member, ones)

    rim_send[:, 0:C] = sums[CELL_DEV : CELL_DEV + 8, :]
    rim_send[:, C : C + 128] = counts[CELL_DEV : CELL_DEV + 8, :]
    rim = remote(rim_send, rim_recv, rim_send_sem, rim_recv_sem, -1)
    rim.start()

    def pooled(total, count):
        count = jnp.maximum(count, 1.0)
        mean = total / jnp.concatenate([count, count], axis=1)
        return gelu(dot(mean.astype(bf16), wpool[...])).astype(bf16)

    out[...] = pooled(sums[:CELL_DEV, :], counts[:CELL_DEV, :])
    rim.wait()
    tail = CELL_DEV - 16
    last = lax.broadcasted_iota(jnp.int32, (16, 1), 0) == 15
    extra = jnp.where(last, rim_recv[0:1, 0:C], 0.0)
    extra_count = jnp.where(last, rim_recv[0:1, C : C + 128], 0.0)
    out[tail:, :] = pooled(
        sums[tail:CELL_DEV, :] + extra, counts[tail:CELL_DEV, :] + extra_count
    )


def on_device(
    points_z,
    patch_len,
    z_dest,
    cell_of,
    norm_gain,
    qkv_weight,
    out_weight,
    up_weight,
    down_weight,
    pool_weight,
):
    n_pts = lax.axis_size("pts")
    devices = lax.axis_size(("grp", "pts"))
    deltas = (3, -3, 2, -2, 1, -1, devices // 2, 0)
    vmem = pl.BlockSpec(memory_space=pltpu.VMEM)
    smem = pl.BlockSpec(memory_space=pltpu.SMEM)
    return pl.pallas_call(
        functools.partial(body, deltas, devices, n_pts),
        out_shape=jax.ShapeDtypeStruct((CELL_DEV, CP), bf16),
        in_specs=[smem, smem] + [pl.BlockSpec(memory_space=pl.ANY)] * 8,
        out_specs=vmem,
        scratch_shapes=[
            pltpu.VMEM((NB, BLK, C), bf16),
            pltpu.VMEM((NB, BLK), jnp.int32),
            pltpu.VMEM((2, 2, C), f32),
            pltpu.VMEM((2, C, 3 * C), bf16),
            pltpu.VMEM((2, C, C), bf16),
            pltpu.VMEM((2, C, FF), bf16),
            pltpu.VMEM((2, FF, C), bf16),
            pltpu.VMEM((C, CP), bf16),
            pltpu.VMEM((PATCH, C), bf16),
            pltpu.VMEM((PATCH, C), bf16),
            pltpu.VMEM((HEADS, 8, QW), f32),
            pltpu.VMEM((PATCH, C), bf16),
            pltpu.VMEM((PATCH, C), bf16),
            pltpu.VMEM((PATCH, C), bf16),
            pltpu.VMEM((2 * C, C), bf16),
            pltpu.VMEM((C, 2 * C), bf16),
            pltpu.VMEM((4, PATCH, 128), f8),
            pltpu.VMEM((HEADS, C, PATCH), f8),
            pltpu.VMEM((HEADS, 2 * HD, PATCH), bf16),
            pltpu.VMEM((C, PATCH), bf16),
            pltpu.VMEM((PATCH, QW), f32),
            pltpu.VMEM((PATCH, QW), f32),
            pltpu.VMEM((8, QW), f32),
            pltpu.VMEM((8, QW), f32),
            pltpu.VMEM((NB, 8, C), jnp.int32),
            pltpu.VMEM((NB, 8, C), jnp.int32),
            pltpu.VMEM((8, C + 128), f32),
            pltpu.VMEM((8, C + 128), f32),
            pltpu.SemaphoreType.DMA((NB,)),
            pltpu.SemaphoreType.DMA((NB,)),
            pltpu.SemaphoreType.DMA((NB,)),
            pltpu.SemaphoreType.DMA((NB,)),
            pltpu.SemaphoreType.DMA,
            pltpu.SemaphoreType.DMA,
            pltpu.SemaphoreType.DMA((8,)),
        ],
        compiler_params=pltpu.CompilerParams(
            collective_id=0, has_side_effects=True, vmem_limit_bytes=60 * 2**20
        ),
        name="encoder",
    )(
        patch_len,
        z_dest,
        points_z.reshape(NB, BLK, C),
        cell_of.reshape(NB, BLK),
        norm_gain,
        qkv_weight,
        out_weight,
        up_weight,
        down_weight,
        pool_weight,
    )


def solution(mesh):
    placed = (
        P(("grp", "pts"), None),
        P(("grp", "pts")),
        P(("grp", "pts")),
        P(("grp", "pts")),
        P(),
        P(),
        P(),
        P(),
        P(),
        P(),
    )
    return jax.shard_map(
        on_device, mesh=mesh, in_specs=placed, out_specs=P(("grp", "pts"), None), check_vma=False
    )
```

```python
import functools

import jax
import jax.numpy as jnp
from jax import lax
from jax.experimental import pallas as pl
from jax.experimental.pallas import tpu as pltpu
from jax.sharding import PartitionSpec as P

C = 256
HEADS = 16
HD = 16
PATCH = 1024
BLK = 128
NB = 8
CELL_DEV = 256
CP = 512
FF = 1024
NORM_EPS = 1e-05
QW = 512
TILES = PATCH // QW
UNROLL = 8
ROWS = 256
LOG2E = 1.4426950408889634
POOL_ROWS = 272
ERF = (
    0.7978281360364785,
    0.03646879080750627,
    -0.00012486153426078468,
    -3.0581026877848916e-05,
    1.1190833948473977e-06,
)
F8_TOP = 400.0
bf16 = jnp.bfloat16
f8 = jnp.float8_e4m3fn
f32 = jnp.float32
MESH = pl.DeviceIdType.MESH


def gelu(x):
    near = x.astype(bf16)
    u = near * near
    r = jnp.full_like(u, ERF[4])
    for coefficient in ERF[3::-1]:
        r = r * u + jnp.asarray(coefficient, bf16)
    half = 0.5 * x
    return half + half * jnp.tanh((near * r).astype(f32))


def norm(x, gain):
    centered = x - jnp.mean(x, axis=-1, keepdims=True)
    variance = jnp.mean(centered * centered, axis=-1, keepdims=True)
    return (centered * lax.rsqrt(variance + NORM_EPS) * gain).astype(bf16)


def dot(a, b):
    return jnp.dot(a, b, preferred_element_type=f32)


def dot_nt(a, b):
    return lax.dot_general(a, b, (((1,), (1,)), ((), ())), preferred_element_type=f32)


def dot_tn(a, b):
    return lax.dot_general(a, b, (((0,), (0,)), ((), ())), preferred_element_type=f32)


def prepare(b, gain, wqkv, wq_t, wk2, sigma):
    reach = 16.1 * jnp.max(jnp.abs(gain[b, 0:1, :]))
    column = lax.broadcasted_iota(jnp.int32, (C, C), 0) // HD
    same_head = (column == lax.broadcasted_iota(jnp.int32, (C, C), 1) // HD).astype(f32).astype(bf16)

    def power(exponent):
        return jnp.exp2(exponent).astype(bf16).astype(f32)

    def exponents(w):
        squares = jnp.sum(w * w, axis=0, keepdims=True)
        squares = jnp.broadcast_to(squares, (16, C)).astype(bf16)
        total = jnp.maximum(dot(squares, same_head)[0:1, :], 1e-30)
        bound = reach * jnp.sqrt(total)
        return jnp.floor(jnp.log(F8_TOP / bound) * LOG2E)

    wq = wqkv[b, :, 0:C].astype(f32)
    wk = wqkv[b, :, C : 2 * C].astype(f32)
    wv = wqkv[b, :, 2 * C : 3 * C].astype(f32)
    q_up, k_up = exponents(wq), exponents(wk)
    wq_t[0:C, :] = (wq * power(q_up)).T.astype(bf16)
    wq_t[C : 2 * C, :] = wv.T.astype(bf16)
    column = lax.broadcasted_iota(jnp.int32, (C, 2 * C), 0)
    wide = lax.broadcasted_iota(jnp.int32, (C, 2 * C), 1)
    twice = (column == (wide // (2 * HD)) * HD + wide % HD).astype(f32).astype(bf16)
    wk2[...] = dot((wk * power(k_up)).astype(bf16), twice).astype(bf16)
    back = power(-q_up - k_up) * (HD**-0.5 * LOG2E)
    for h in range(HEADS):
        sigma[h] = jnp.broadcast_to(back[:, h * HD : h * HD + 1], (8, QW))


def project(b, chunk, xs, meta, gain, wq_t, wk2, kk, qt, vt):
    rows = pl.ds(chunk * ROWS, ROWS)
    xn = norm(xs[rows, :].astype(f32), gain[b, 0:1, :])
    k = dot(xn, wk2[...]).astype(bf16).astype(f32)
    is_high = lax.broadcasted_iota(jnp.int32, (BLK, 2 * C), 1) % (2 * HD) < HD
    for part in range(2):
        slot = chunk * 2 + part
        limit = meta[slot, 1:2, :]
        limit = jnp.concatenate([limit, limit], axis=1)
        live = lax.broadcasted_iota(jnp.int32, (BLK, 2 * C), 0) < limit
        piece = k[part * BLK : (part + 1) * BLK, :]
        piece = jnp.where(live, piece, piece[0:1, :])
        high = piece.astype(f8).astype(f32)
        piece = jnp.where(is_high, high, piece - high).astype(f8)
        for g in range(4):
            kk[g, pl.ds(slot * BLK, BLK), :] = piece[:, g * 128 : (g + 1) * 128]
    qv = dot_nt(wq_t[...], xn)
    q = qv[:C, :].astype(bf16).astype(f32)
    high = q.astype(f8).astype(f32)
    low = q - high
    for h in range(HEADS):
        r = (h % 4) * 2 * HD
        at = slice(h * HD, (h + 1) * HD)
        qt[h, r : r + 2 * HD, rows] = jnp.concatenate([high[at], high[at]], axis=0).astype(f8)
        qt[h, 128 + r : 128 + r + 2 * HD, rows] = jnp.concatenate(
            [low[at], low[at]], axis=0
        ).astype(f8)
    limits = jnp.concatenate(
        [meta[chunk * 2, 1:2, 0:BLK], meta[chunk * 2 + 1, 1:2, 0:BLK]], axis=1
    )
    lane = lax.broadcasted_iota(jnp.int32, (1, ROWS), 1) % BLK
    live_row = (lane < limits).astype(f32)
    v = (qv[C:, :] * live_row).astype(bf16)
    first = lax.broadcasted_iota(jnp.int32, (HD, ROWS), 0) == 0
    ones = jnp.where(first, live_row, 0.0).astype(bf16)
    for h in range(HEADS):
        vt[h, 0:HD, rows] = v[h * HD : (h + 1) * HD, :]
        vt[h, HD : 2 * HD, rows] = ones


def scores(step, kk, qt, sigma, s, m):
    h, t = step % HEADS, step // HEADS
    keys = kk[h // 4]
    queries = qt[h, :, pl.ds(pl.multiple_of(t * QW, QW), QW)]
    raw = dot(jnp.concatenate([keys, keys], axis=1), queries) * sigma[h][0:1, :]
    s[...] = raw
    m[...] = jnp.max(raw.reshape(PATCH // 8, 8, QW), axis=0)


def values(h, t, vt, ot, s, m):
    top = jnp.max(m[...], axis=0, keepdims=True)
    total = None
    for c in range(PATCH // 256):
        keys = pl.ds(c * 256, 256)
        e = jnp.exp2(s[keys, :] - top).astype(bf16)
        part = dot(vt[h, :, keys], e)
        total = part if total is None else total + part
    ot[pl.ds(pl.multiple_of(h * HD, HD), HD), pl.ds(t * QW, QW)] = (
        total[0:HD, :] / total[HD : HD + 1, :]
    ).astype(bf16)


def attention(t, kk, qt, vt, ot, sigma, s_a, s_b, m_a, m_b):
    if t == 0:
        scores(0, kk, qt, sigma, s_a, m_a)

    def group(n, carry):
        for o in range(0, UNROLL, 2):
            h = UNROLL * n + o
            step = t * HEADS + h
            scores(step + 1, kk, qt, sigma, s_b, m_b)
            values(h, t, vt, ot, s_a, m_a)
            scores(jnp.minimum(step + 2, TILES * HEADS - 1), kk, qt, sigma, s_a, m_a)
            values(h + 1, t, vt, ot, s_b, m_b)
        return carry

    lax.fori_loop(0, HEADS // UNROLL, group, 0)


def residual(b, chunk, xs, gain, ot, wo, hs, hns):
    rows = pl.ds(chunk * ROWS, ROWS)
    h = (xs[rows, :].astype(f32) + dot_tn(ot[:, rows], wo[b])).astype(bf16)
    hs[rows, :] = h
    hns[rows, :] = norm(h.astype(f32), gain[b, 1:2, :])


def feed_forward(b, chunk, hs, hns, wup, wdown):
    rows = pl.ds(chunk * ROWS, ROWS)
    u = gelu(dot(hns[rows, :], wup[b])).astype(bf16)
    return (hs[rows, :].astype(f32) + dot(u, wdown[b])).astype(bf16)


def body(
    deltas,
    devices,
    n_pts,
    patch_len,
    z_dest,
    x_hbm,
    cells_hbm,
    gain_hbm,
    wqkv_hbm,
    wo_hbm,
    wup_hbm,
    wdown_hbm,
    wpool_hbm,
    out,
    x_ref,
    cells,
    gain,
    wqkv,
    wo,
    wup,
    wdown,
    wpool,
    hs,
    hns,
    sigma,
    x_first,
    x_second,
    y_send,
    wq_t,
    wk2,
    kk,
    qt,
    vt,
    ot,
    s_a,
    s_b,
    m_a,
    m_b,
    meta_send,
    meta_recv,
    rim_send,
    rim_recv,
    send_sem,
    recv_sem,
    meta_send_sem,
    meta_recv_sem,
    rim_send_sem,
    rim_recv_sem,
    load_sem,
    most,
    rest,
):
    loads = [
        pltpu.make_async_copy(src, dst, load_sem.at[n])
        for n, (src, dst) in enumerate(
            (
                (x_hbm, x_ref),
                (gain_hbm, gain),
                (wqkv_hbm, wqkv),
                (wo_hbm, wo),
                (wup_hbm, wup),
                (wdown_hbm, wdown),
                (cells_hbm, cells),
                (wpool_hbm, wpool),
            )
        )
    ]
    for load in loads:
        load.start()
    me = lax.axis_index("grp") * n_pts + lax.axis_index("pts")

    def device(delta):
        flat = (me + delta + devices) % devices
        return (flat // n_pts, flat % n_pts)

    barrier = pltpu.get_barrier_semaphore()
    for delta in deltas:
        if delta:
            pl.semaphore_signal(barrier, inc=1, device_id=device(delta), device_id_type=MESH)

    def remote(src, dst, ssem, rsem, delta):
        return pltpu.make_async_remote_copy(
            src_ref=src, dst_ref=dst, send_sem=ssem, recv_sem=rsem,
            device_id=device(delta), device_id_type=MESH,
        )

    def block_copy(slot):
        rows = pl.ds(slot * BLK, BLK)
        return remote(
            y_send.at[rows], x_second.at[rows], send_sem.at[slot], recv_sem.at[slot], deltas[slot]
        )

    def meta_copy(slot):
        return remote(
            meta_send.at[slot], meta_recv.at[slot], meta_send_sem.at[slot],
            meta_recv_sem.at[slot], deltas[slot],
        )

    qt[...] = jnp.zeros_like(qt)
    for load in loads[:3]:
        load.wait()
    row = lax.broadcasted_iota(jnp.int32, (8, C), 0)
    for slot, delta in enumerate(deltas):
        base = ((me + delta + devices) % devices) * NB
        block = jnp.int32(0)
        place = jnp.int32(0)
        for n in range(NB):
            offset = z_dest[n] - base
            hit = jnp.logical_and(offset >= 0, offset < NB)
            block = block + jnp.where(hit, n, 0)
            place = place + jnp.where(hit, offset, 0)
        block = jnp.minimum(block, NB - 1)
        x_first[pl.ds(slot * BLK, BLK), :] = x_ref[block]
        limit = patch_len[0] - block * BLK
        meta = jnp.where(row == 1, limit, place)
        meta_send[slot] = meta
        if delta == 0:
            meta_recv[slot] = meta
    chunks = PATCH // ROWS
    prepare(0, gain, wqkv, wq_t, wk2, sigma)
    for chunk in range(chunks):
        project(0, chunk, x_first, meta_send, gain, wq_t, wk2, kk, qt, vt)
    pl.semaphore_wait(barrier, NB - 1)
    for slot, delta in enumerate(deltas):
        if delta:
            meta_copy(slot).start()
    per_tile = chunks // TILES
    for t in range(TILES):
        attention(t, kk, qt, vt, ot, sigma, s_a, s_b, m_a, m_b)
        if t == 0:
            for load in loads[3:]:
                load.wait()
        mine = range(t * per_tile, (t + 1) * per_tile)
        for chunk in mine:
            residual(0, chunk, x_first, gain, ot, wo, hs, hns)
        for chunk in mine:
            y = feed_forward(0, chunk, hs, hns, wup, wdown)
            for part in range(2):
                slot = chunk * 2 + part
                rows = pl.ds(slot * BLK, BLK)
                piece = y[part * BLK : (part + 1) * BLK, :]
                if deltas[slot]:
                    y_send[rows, :] = piece
                    block_copy(slot).start()
                else:
                    x_second[rows, :] = piece

    prepare(1, gain, wqkv, wq_t, wk2, sigma)
    for slot, delta in enumerate(deltas):
        if delta:
            meta_copy(slot).wait()
    for chunk in range(chunks):
        for slot in (chunk * 2, chunk * 2 + 1):
            if deltas[slot]:
                block_copy(slot).wait()
        project(1, chunk, x_second, meta_recv, gain, wq_t, wk2, kk, qt, vt)
    for t in range(TILES):
        attention(t, kk, qt, vt, ot, sigma, s_a, s_b, m_a, m_b)
    for chunk in range(chunks):
        residual(1, chunk, x_second, gain, ot, wo, hs, hns)

    number = lax.broadcasted_iota(jnp.int32, (POOL_ROWS, BLK), 0)
    wanted = jnp.where(number == CELL_DEV, -1, jnp.where(number > CELL_DEV, -5, number))
    lane = lax.broadcasted_iota(jnp.int32, (1, BLK), 1)
    ones = jnp.ones((ROWS, 128), bf16)
    sums = jnp.zeros((POOL_ROWS, C), f32)
    counts = jnp.zeros((POOL_ROWS, 128), f32)
    for chunk in range(chunks):
        y = feed_forward(1, chunk, hs, hns, wup, wdown)
        members = []
        for slot in (chunk * 2, chunk * 2 + 1):
            place = meta_recv[slot, 0:1, 0:BLK]
            cell = jnp.zeros((1, BLK), jnp.int32)
            for n in range(NB):
                cell = cell + jnp.where(place == n, cells[n : n + 1, :], 0)
            cell = jnp.where(lane < meta_recv[slot, 1:2, 0:BLK], cell - me * CELL_DEV, -9)
            members.append((cell == wanted).astype(f32).astype(bf16))
        member = jnp.concatenate(members, axis=1)
        sums = sums + dot(member, y)
        counts = counts + dot(member, ones)

    rim_send[:, 0:C] = sums[CELL_DEV : CELL_DEV + 8, :]
    rim_send[:, C : C + 128] = counts[CELL_DEV : CELL_DEV + 8, :]
    rim = remote(rim_send, rim_recv, rim_send_sem, rim_recv_sem, -1)
    rim.start()

    def pooled(total, count):
        count = jnp.maximum(count, 1.0)
        mean = total / jnp.concatenate([count, count], axis=1)
        return gelu(dot(mean.astype(bf16), wpool[...])).astype(bf16)

    tail = CELL_DEV - 16
    most[...] = pooled(sums[:tail, :], counts[:tail, :])
    store_most = pltpu.make_async_copy(most, out.at[pl.ds(0, tail)], load_sem.at[0])
    store_most.start()
    rim.wait()
    last = lax.broadcasted_iota(jnp.int32, (16, 1), 0) == 15
    extra = jnp.where(last, rim_recv[0:1, 0:C], 0.0)
    extra_count = jnp.where(last, rim_recv[0:1, C : C + 128], 0.0)
    rest[...] = pooled(
        sums[tail:CELL_DEV, :] + extra, counts[tail:CELL_DEV, :] + extra_count
    )
    store_rest = pltpu.make_async_copy(rest, out.at[pl.ds(tail, 16)], load_sem.at[1])
    store_rest.start()
    store_rest.wait()
    store_most.wait()


def on_device(
    points_z,
    patch_len,
    z_dest,
    cell_of,
    norm_gain,
    qkv_weight,
    out_weight,
    up_weight,
    down_weight,
    pool_weight,
):
    n_pts = lax.axis_size("pts")
    devices = lax.axis_size(("grp", "pts"))
    deltas = (3, -3, 2, -2, 1, -1, devices // 2, 0)
    smem = pl.BlockSpec(memory_space=pltpu.SMEM)
    return pl.pallas_call(
        functools.partial(body, deltas, devices, n_pts),
        out_shape=jax.ShapeDtypeStruct((CELL_DEV, CP), bf16),
        in_specs=[smem, smem] + [pl.BlockSpec(memory_space=pl.ANY)] * 8,
        out_specs=pl.BlockSpec(memory_space=pl.ANY),
        scratch_shapes=[
            pltpu.VMEM((NB, BLK, C), bf16),
            pltpu.VMEM((NB, BLK), jnp.int32),
            pltpu.VMEM((2, 2, C), f32),
            pltpu.VMEM((2, C, 3 * C), bf16),
            pltpu.VMEM((2, C, C), bf16),
            pltpu.VMEM((2, C, FF), bf16),
            pltpu.VMEM((2, FF, C), bf16),
            pltpu.VMEM((C, CP), bf16),
            pltpu.VMEM((PATCH, C), bf16),
            pltpu.VMEM((PATCH, C), bf16),
            pltpu.VMEM((HEADS, 8, QW), f32),
            pltpu.VMEM((PATCH, C), bf16),
            pltpu.VMEM((PATCH, C), bf16),
            pltpu.VMEM((PATCH, C), bf16),
            pltpu.VMEM((2 * C, C), bf16),
            pltpu.VMEM((C, 2 * C), bf16),
            pltpu.VMEM((4, PATCH, 128), f8),
            pltpu.VMEM((HEADS, C, PATCH), f8),
            pltpu.VMEM((HEADS, 2 * HD, PATCH), bf16),
            pltpu.VMEM((C, PATCH), bf16),
            pltpu.VMEM((PATCH, QW), f32),
            pltpu.VMEM((PATCH, QW), f32),
            pltpu.VMEM((8, QW), f32),
            pltpu.VMEM((8, QW), f32),
            pltpu.VMEM((NB, 8, C), jnp.int32),
            pltpu.VMEM((NB, 8, C), jnp.int32),
            pltpu.VMEM((8, C + 128), f32),
            pltpu.VMEM((8, C + 128), f32),
            pltpu.SemaphoreType.DMA((NB,)),
            pltpu.SemaphoreType.DMA((NB,)),
            pltpu.SemaphoreType.DMA((NB,)),
            pltpu.SemaphoreType.DMA((NB,)),
            pltpu.SemaphoreType.DMA,
            pltpu.SemaphoreType.DMA,
            pltpu.SemaphoreType.DMA((8,)),
            pltpu.VMEM((CELL_DEV - 16, CP), bf16),
            pltpu.VMEM((16, CP), bf16),
        ],
        compiler_params=pltpu.CompilerParams(
            collective_id=0, has_side_effects=True, vmem_limit_bytes=60 * 2**20
        ),
        name="encoder",
    )(
        patch_len,
        z_dest,
        points_z.reshape(NB, BLK, C),
        cell_of.reshape(NB, BLK),
        norm_gain,
        qkv_weight,
        out_weight,
        up_weight,
        down_weight,
        pool_weight,
    )


def solution(mesh):
    placed = (
        P(("grp", "pts"), None),
        P(("grp", "pts")),
        P(("grp", "pts")),
        P(("grp", "pts")),
        P(),
        P(),
        P(),
        P(),
        P(),
        P(),
    )
    return jax.shard_map(
        on_device, mesh=mesh, in_specs=placed, out_specs=P(("grp", "pts"), None), check_vma=False
    )
```
